512 devices in a mesh: section: 16 (over y, core), dom: 32 (over z, x).
Axes of the slice: x: 4, y: 8, z: 8, core: 2. Of those that a mesh axis runs over, the one named last changes fastest.
Arguments:
- right_sides: float32 [4096, 32, 128], P(('section', 'dom')), may hold values from -6 to 6
- diag_inverse: bfloat16 [4096, 128, 128], P(('section', 'dom')), as said below
- diag_blocks: bfloat16 [4096, 128, 128], P(('section', 'dom')), as said below
- lower_blocks: bfloat16 [4096, 3, 128, 128], P(('section', 'dom'))
- upper_blocks: bfloat16 [4096, 3, 128, 128], P(('section', 'dom'))
- halo_blocks: bfloat16 [4096, 2, 128, 128], P(('section', 'dom')), may hold values from -0.1875 to 0.1875
- lower_index: int32 [4096, 3], P(('section', 'dom')), may hold values from 0 to 7, as said below
- upper_index: int32 [4096, 3], P(('section', 'dom')), may hold values from 0 to 7, as said below
- halo_index: int32 [4096, 2], P(('section', 'dom')), may hold values from 0 to 7, as said below
Outputs:
- solution: float32 [4096, 32, 128], P(('section', 'dom'))
- product: float32 [4096, 32, 128], P(('section', 'dom'))
The draws below stay inside these ranges and needn't reach their ends.
Inputs may be any that keep to these rules, and one draw needn't show every extreme that they name: `lower_index`: for block row g with k = g mod 8, every entry lies in 0 to k, and the first entry equals k. `upper_index`: for block row g with k = g mod 8, every entry lies in k to 7, and the first entry equals k. `halo_index`: for block row g the first entry equals g mod 8. `diag_inverse`: each block is the identity scaled row by row plus a full block. `diag_blocks`: each block is the identity scaled row by row plus a full block.
All inputs are finite; a program needn't handle non-finite values.
Results may differ from the reference program's by a relative error of at most 0.029.
Values may be sent and summed in bfloat16 or wider, within the bound.
A program may use at most 64 MiB of HBM per device.

```python
import math
import jax
import jax.numpy as jnp
from jax import lax

BLK = 128
NRHS = 32
ROWS_DEV = 8
NLOW = 3
NUPP = 3
NHALO = 2
RIM = 4
BROWS = 4096
N_SECTION = 16
N_DOM = 32


def draw_diag_inverse(key, part):
    key_diag, key_jitter = jax.random.split(jax.random.fold_in(key, 11))
    diagonal = jax.random.uniform(key_diag, (BROWS, BLK), jnp.float32, 0.7, 1.3)
    jitter = jax.random.normal(key_jitter, (BROWS, BLK, BLK), jnp.float32)
    identity = jnp.eye(BLK, dtype=jnp.float32)
    return (jitter * (0.35 / math.sqrt(BLK)) + diagonal[:, :, None] * identity).astype(jnp.bfloat16)


def draw_diag_blocks(key, part):
    key_diag, key_jitter = jax.random.split(jax.random.fold_in(key, 23))
    diagonal = jax.random.uniform(key_diag, (BROWS, BLK), jnp.float32, 0.8, 1.6)
    jitter = jax.random.normal(key_jitter, (BROWS, BLK, BLK), jnp.float32)
    identity = jnp.eye(BLK, dtype=jnp.float32)
    return (jitter * (0.35 / math.sqrt(BLK)) + diagonal[:, :, None] * identity).astype(jnp.bfloat16)


def slot_blocks(key, slots):
    jitter = jax.random.normal(key, (BROWS, slots, BLK, BLK), jnp.float32)
    weights = jnp.where(jnp.arange(slots) == 0, 0.7, 0.35).astype(jnp.float32)
    return (jitter * weights[None, :, None, None] / math.sqrt(BLK)).astype(jnp.bfloat16)


def draw_lower_blocks(key, part):
    return slot_blocks(jax.random.fold_in(key, 37), NLOW)


def draw_upper_blocks(key, part):
    return slot_blocks(jax.random.fold_in(key, 41), NUPP)


def draw_lower_index(key, part):
    position = jnp.arange(BROWS, dtype=jnp.int32) % ROWS_DEV
    others = jax.random.randint(jax.random.fold_in(key, 53), (BROWS, NLOW - 1), 0, (position + 1)[:, None], dtype=jnp.int32)
    return jnp.concatenate([position[:, None], others], axis=1)


def draw_upper_index(key, part):
    position = jnp.arange(BROWS, dtype=jnp.int32) % ROWS_DEV
    others = jax.random.randint(jax.random.fold_in(key, 59), (BROWS, NUPP - 1), position[:, None], ROWS_DEV, dtype=jnp.int32)
    return jnp.concatenate([position[:, None], others], axis=1)


def draw_halo_index(key, part):
    position = jnp.arange(BROWS, dtype=jnp.int32) % ROWS_DEV
    others = jax.random.randint(jax.random.fold_in(key, 61), (BROWS, NHALO - 1), 0, 2 * RIM, dtype=jnp.int32)
    return jnp.concatenate([(position % (2 * RIM))[:, None], others], axis=1)


def shard_levels(stream_key, dims, cuts, least, high):
    def one(dim, shards_of):
        steps = jax.random.uniform(jax.random.fold_in(jax.random.fold_in(stream_key, 6), dim), (shards_of,), jnp.float32, least / len(cuts), high / len(cuts))
        return jnp.repeat(jnp.exp(steps), dims[dim] // shards_of).reshape((-1,) + (1,) * (len(dims) - dim - 1))

    gain = one(*cuts[0])
    for cut in cuts[1:]:
        gain = gain * one(*cut)
    return gain


def bell_draw(own_key, dims, width, most, shards=(), kind=jnp.bfloat16):
    loudness = shard_levels(own_key, dims, shards, -0.22, 0.18) if shards else 1.0
    values = jax.random.normal(own_key, dims, jnp.float32) * width * loudness
    return jnp.minimum(jnp.maximum(values, -most), most).astype(kind)


def setup_inputs(seed: int = 0) -> dict:
    key_of = jax.random.split(jax.random.key(seed), 10)
    return {
        "right_sides": bell_draw(key_of[0], (BROWS, NRHS, BLK), 1.0, 6.0, ((0, 512),), jnp.float32),
        "diag_inverse": draw_diag_inverse(jax.random.fold_in(key_of[9], 71), 0),
        "diag_blocks": draw_diag_blocks(jax.random.fold_in(key_of[9], 71), 0),
        "lower_blocks": draw_lower_blocks(jax.random.fold_in(key_of[9], 71), 0),
        "upper_blocks": draw_upper_blocks(jax.random.fold_in(key_of[9], 71), 0),
        "halo_blocks": bell_draw(key_of[5], (BROWS, NHALO, BLK, BLK), (8 * BLK) ** -0.5, 0.1875, ((0, 512),)),
        "lower_index": draw_lower_index(jax.random.fold_in(key_of[9], 71), 0),
        "upper_index": draw_upper_index(jax.random.fold_in(key_of[9], 71), 0),
        "halo_index": draw_halo_index(jax.random.fold_in(key_of[9], 71), 0),
    }


highest = lax.Precision.HIGHEST


def solve_down(target, inverse, lower_part, pointers, inflow):
    def advance(solved, entries):
        target_row, inverse_row, blocks, chosen, position = entries
        picked = jnp.take(solved, chosen, axis=0)
        source = jnp.where((chosen == position)[:, None, None], inflow[None], picked)
        source = source.astype(jnp.bfloat16).astype(jnp.float32)
        summed = jnp.einsum("sqb,sbc->qc", source, blocks.astype(jnp.float32), precision=highest)
        gap = (target_row - summed).astype(jnp.bfloat16)
        result = jnp.dot(gap, inverse_row, preferred_element_type=jnp.float32)
        return lax.dynamic_update_index_in_dim(solved, result, position, 0), None

    positions = jnp.arange(target.shape[0], dtype=jnp.int32)
    solved, unused = lax.scan(advance, jnp.zeros_like(target), (target, inverse, lower_part, pointers, positions))
    return solved


def solve_up(target, inverse, upper_part, pointers, inflow):
    def advance(solved, entries):
        target_row, inverse_row, blocks, chosen, position = entries
        picked = jnp.take(solved, chosen, axis=0)
        source = jnp.where((chosen == position)[:, None, None], inflow[None], picked)
        source = source.astype(jnp.bfloat16).astype(jnp.float32)
        summed = jnp.einsum("sqb,sbc->qc", source, blocks.astype(jnp.float32), precision=highest)
        result = target_row - jnp.dot(summed.astype(jnp.bfloat16), inverse_row, preferred_element_type=jnp.float32)
        return lax.dynamic_update_index_in_dim(solved, result, position, 0), None

    positions = jnp.arange(target.shape[0], dtype=jnp.int32)
    solved, unused = lax.scan(advance, jnp.zeros_like(target), (target, inverse, upper_part, pointers, positions), reverse=True)
    return solved


def apply_rows(solution, diag_part, lower_part, lower_pointers, upper_part, upper_pointers, halo_part, halo_pointers, before, after, rim_rows):
    positions = jnp.arange(solution.shape[0], dtype=jnp.int32)[:, None]
    lower_source = jnp.where((lower_pointers == positions)[:, :, None, None], before[None, None], jnp.take(solution, lower_pointers, axis=0))
    upper_source = jnp.where((upper_pointers == positions)[:, :, None, None], after[None, None], jnp.take(solution, upper_pointers, axis=0))
    halo_source = jnp.take(rim_rows, halo_pointers, axis=0)
    total = jnp.einsum("rqb,rbc->rqc", solution.astype(jnp.float32), diag_part.astype(jnp.float32), precision=highest)
    total = total + jnp.einsum("rsqb,rsbc->rqc", lower_source.astype(jnp.float32), lower_part.astype(jnp.float32), precision=highest)
    total = total + jnp.einsum("rsqb,rsbc->rqc", upper_source.astype(jnp.float32), upper_part.astype(jnp.float32), precision=highest)
    total = total + jnp.einsum("rsqb,rsbc->rqc", halo_source.astype(jnp.float32), halo_part.astype(jnp.float32), precision=highest)
    return total


def by_device(array):
    return array.reshape((N_SECTION, N_DOM, ROWS_DEV) + array.shape[1:])


def reference(right_sides, diag_inverse, diag_blocks, lower_blocks, upper_blocks, halo_blocks, lower_index, upper_index, halo_index):
    targets = by_device(right_sides)
    inverses = by_device(diag_inverse)
    diagonals = by_device(diag_blocks)
    lowers = by_device(lower_blocks)
    uppers = by_device(upper_blocks)
    halos = by_device(halo_blocks)
    lower_ptrs = by_device(lower_index)
    upper_ptrs = by_device(upper_index)
    halo_ptrs = by_device(halo_index)
    zeros = jnp.zeros((N_DOM, NRHS, BLK), right_sides.dtype)

    def forward_section(inflow, entries):
        solved = jax.vmap(solve_down)(*entries, inflow)
        return solved[:, -1], solved

    unused, forward = lax.scan(forward_section, zeros, (targets, inverses, lowers, lower_ptrs))

    def backward_section(inflow, entries):
        solved = jax.vmap(solve_up)(*entries, inflow)
        return solved[:, 0], solved

    unused, solution = lax.scan(backward_section, zeros, (forward, inverses, uppers, upper_ptrs), reverse=True)
    rounded = solution.astype(jnp.bfloat16)
    last_rows = rounded[:, :, -1]
    first_rows = rounded[:, :, 0]
    before = jnp.concatenate([jnp.zeros_like(last_rows[:1]), last_rows[:-1]], axis=0)
    after = jnp.concatenate([first_rows[1:], jnp.zeros_like(first_rows[:1])], axis=0)
    left_rim = jnp.concatenate([jnp.zeros_like(rounded[:, :1, ROWS_DEV - RIM:]), rounded[:, :-1, ROWS_DEV - RIM:]], axis=1)
    right_rim = jnp.concatenate([rounded[:, 1:, :RIM], jnp.zeros_like(rounded[:, :1, :RIM])], axis=1)
    rim_rows = jnp.concatenate([left_rim, right_rim], axis=2)
    product = lax.map(lambda entries: jax.vmap(apply_rows)(*entries), (rounded, diagonals, lowers, lower_ptrs, uppers, upper_ptrs, halos, halo_ptrs, before, after, rim_rows))
    return solution.reshape(right_sides.shape), product.reshape(right_sides.shape)
```

```python
import functools

import jax
import jax.numpy as jnp
from jax import lax
from jax.experimental import pallas as pl
from jax.experimental.pallas import tpu as pltpu
from jax.sharding import PartitionSpec as P

F32 = jnp.float32
BF16 = jnp.bfloat16
MESH = pl.DeviceIdType.MESH
ROWS = 8
BLK = 128
NRHS = 32
RIM = 4
AFFINE = BLK + NRHS
WIDE = AFFINE + BLK
ELEMENT = AFFINE + WIDE
PIECES = ((0, AFFINE), (AFFINE, 2 * AFFINE), (2 * AFFINE, ELEMENT))


def dot(left, right):
    return jnp.dot(left.astype(BF16), right, preferred_element_type=F32)


def joined(left, right):
    right_m, right_a = right[:BLK], right[BLK:AFFINE]
    right_h, right_b = right[AFFINE : AFFINE + BLK], right[AFFINE + BLK : 2 * AFFINE]
    right_k, left_k = right[2 * AFFINE :], left[2 * AFFINE :]
    through = dot(left[:AFFINE], jnp.concatenate([right_m, right_h], axis=1))
    onward = jnp.concatenate(
        [through[:BLK, :BLK], through[BLK:, :BLK] + right_a.astype(F32)], axis=0
    )
    back = jnp.concatenate(
        [
            through[:BLK, BLK:].astype(BF16),
            (through[BLK:, BLK:] + right_b.astype(F32)).astype(BF16),
            right_k,
        ],
        axis=0,
    )
    back = dot(back, left_k)
    back = jnp.concatenate(
        [back[:AFFINE] + left[AFFINE : 2 * AFFINE].astype(F32), back[AFFINE:]], axis=0
    )
    return onward.astype(BF16), back.astype(BF16)


def kernel(
    sections,
    parts,
    lower_index,
    upper_index,
    halo_index,
    rhs_hbm,
    inverse_hbm,
    diag_hbm,
    lower_hbm,
    upper_hbm,
    halo_hbm,
    solution_ref,
    product_ref,
    rhs,
    inverse,
    diag,
    lower,
    upper,
    halo,
    fwd,
    fwd_wide,
    bwd,
    bwd_values,
    pair,
    ring,
    ends,
    last_own,
    last_in,
    rows,
    rim,
    load_sem,
    pair_send,
    pair_recv,
    ring_send,
    ring_recv,
    ends_send,
    ends_recv,
    last_send,
    last_recv,
    rim_send,
    rim_recv,
):
    chips = sections // 2
    left_hops = chips // 2
    right_hops = chips - 1 - left_hops
    section = lax.axis_index("section")
    part = lax.axis_index("dom")
    core = lax.rem(section, 2)
    chip = lax.div(section, 2)
    sibling = (section + 1 - 2 * core, part)
    onto = (2 * lax.rem(chip + 1 - 2 * core + chips, chips) + core, part)
    other = (2 * lax.rem(chip + 2 * core - 1 + chips, chips) + core, part)
    following = (lax.rem(section + 1, sections), part)
    beyond = (lax.rem(section + 2 * core - 1 + sections, sections), part)
    part_up = (section, lax.rem(part + 1, parts))
    part_down = (section, lax.rem(part + parts - 1, parts))

    loads = []
    for place, (source, target) in enumerate(
        (
            (lower_hbm, lower),
            (inverse_hbm, inverse),
            (rhs_hbm, rhs),
            (upper_hbm, upper),
            (diag_hbm, diag),
            (halo_hbm, halo),
        )
    ):
        copy = pltpu.make_async_copy(source, target, load_sem.at[place])
        copy.start()
        loads.append(copy)

    barrier = pltpu.get_barrier_semaphore()
    for device in (sibling, onto, other, beyond, part_up, part_down):
        pl.semaphore_signal(barrier, inc=1, device_id=device, device_id_type=MESH)

    spread = lax.broadcasted_iota(jnp.int32, (BLK, BLK), 0)
    identity = (spread == lax.broadcasted_iota(jnp.int32, (BLK, BLK), 1)).astype(F32)
    has_before = (section > 0).astype(F32)
    has_after = (section < sections - 1).astype(F32)
    fwd[ROWS, :BLK] = (identity * has_before).astype(BF16)
    fwd[ROWS, BLK:] = jnp.zeros((NRHS, BLK), BF16)
    bwd[ROWS, :AFFINE] = jnp.zeros((AFFINE, BLK), BF16)
    bwd[ROWS, AFFINE:] = (identity * has_after).astype(BF16)

    for copy in loads[:3]:
        copy.wait()
    for k in range(ROWS):
        folded = dot(lower[k].reshape(3 * BLK, BLK), inverse[k])
        base = jnp.concatenate([folded[:BLK] * -has_before, dot(rhs[k], inverse[k])], axis=0)
        slots = [jnp.where(lower_index[k, m] == k, ROWS, lower_index[k, m]) for m in (1, 2)]
        sources = jnp.concatenate([fwd[slot] for slot in slots], axis=1)
        wide = base - dot(sources, folded[BLK:].astype(BF16))
        fwd_wide[k] = wide
        fwd[k] = wide.astype(BF16)
    pair[core, :AFFINE] = fwd[ROWS - 1]

    pl.semaphore_wait(barrier, 6)

    def pair_copy(piece, low, high):
        return pltpu.make_async_remote_copy(
            src_ref=pair.at[core, pl.ds(low, high - low)],
            dst_ref=pair.at[core, pl.ds(low, high - low)],
            send_sem=pair_send.at[piece],
            recv_sem=pair_recv.at[piece],
            device_id=sibling,
            device_id_type=MESH,
        )

    pair_onward = pair_copy(0, 0, AFFINE)
    pair_back = pair_copy(1, AFFINE, ELEMENT)
    pair_onward.start()

    loads[3].wait()
    for k in range(ROWS - 1, -1, -1):
        folded = dot(upper[k].reshape(3 * BLK, BLK), inverse[k])
        if k == ROWS - 1:
            last_own[...] = (folded[:BLK] + folded[BLK : 2 * BLK] + folded[2 * BLK :]).astype(BF16)
            last_copy = pltpu.make_async_remote_copy(
                src_ref=last_own,
                dst_ref=last_in,
                send_sem=last_send.at[0],
                recv_sem=last_recv.at[0],
                device_id=following,
                device_id_type=MESH,
            )
            last_copy.start()
        base = jnp.concatenate([fwd_wide[k], folded[:BLK] * -has_after], axis=0)
        slots = [jnp.where(upper_index[k, m] == k, ROWS, upper_index[k, m]) for m in (1, 2)]
        sources = jnp.concatenate([bwd[slot] for slot in slots], axis=1)
        wide = base - dot(sources, folded[BLK:].astype(BF16))
        bwd_values[k] = wide[BLK:AFFINE]
        bwd[k] = wide.astype(BF16)
    pair[core, AFFINE:] = bwd[0]
    pair_back.start()
    pair_onward.wait_recv()
    pair_back.wait_recv()
    onward, back = joined(pair[0], pair[1])
    ring[0, :AFFINE] = onward
    ring[0, AFFINE:] = back

    def ring_copy(hop, piece):
        low, high = PIECES[piece]
        return pltpu.make_async_remote_copy(
            src_ref=ring.at[hop, pl.ds(low, high - low)],
            dst_ref=ring.at[hop + 1, pl.ds(low, high - low)],
            send_sem=ring_send.at[hop, piece],
            recv_sem=ring_recv.at[hop, piece],
            device_id=onto,
            device_id_type=MESH,
        )

    for piece in range(len(PIECES)):
        ring_copy(0, piece).start()

    def take(hop, last):
        for piece in range(len(PIECES)):
            ring_copy(hop - 1, piece).wait_recv()
            if not last:
                ring_copy(hop, piece).start()

    def fold(hop, target, place):
        done = 1 if hop == 2 else left_hops + 1
        left = ring[jnp.where(core == 0, hop, done)]
        right = ring[jnp.where(core == 0, done, hop)]
        onward, back = joined(left, right)
        target[place, :AFFINE] = onward
        target[place, AFFINE:] = back

    for hop in range(1, right_hops):
        take(hop, False)
        if hop >= 2:
            fold(hop, ring, left_hops + 1)

    @pl.when(core == 0)
    def _():
        for hop in range(right_hops, left_hops + 1):
            take(hop, hop == left_hops)
            if hop == left_hops:
                fold(hop, ends, 0)
            elif hop >= 2:
                fold(hop, ring, left_hops + 1)

    @pl.when(core == 1)
    def _():
        take(right_hops, True)
        if right_hops >= 2:
            fold(right_hops, ends, 1)
        else:
            ends[1] = ring[1]

    ends_copy = pltpu.make_async_remote_copy(
        src_ref=ends.at[core],
        dst_ref=ends.at[core],
        send_sem=ends_send.at[0],
        recv_sem=ends_recv.at[0],
        device_id=sibling,
        device_id_type=MESH,
    )
    ends_copy.start()
    ends_copy.wait_recv()

    def value(ref, place, low, size):
        return ref[place, low : low + size]

    inflow = value(ends, 0, BLK, NRHS).astype(F32) + dot(
        value(ends, 1, BLK, NRHS), value(ends, 0, 0, BLK)
    )
    middle = value(pair, 0, BLK, NRHS).astype(F32) + dot(inflow, value(pair, 0, 0, BLK))
    outgoing = value(pair, 1, BLK, NRHS).astype(F32) + dot(middle, value(pair, 1, 0, BLK))
    far = value(ends, 1, BLK, NRHS).astype(F32) + dot(outgoing, value(ends, 1, 0, BLK))
    near = dot(outgoing, value(ends, 1, AFFINE, BLK))
    far = value(ends, 0, AFFINE + BLK, NRHS).astype(F32) + dot(far, value(ends, 0, AFFINE, BLK))
    outflow = (
        value(ends, 1, AFFINE + BLK, NRHS).astype(F32)
        + near
        + dot(far, value(ends, 1, 2 * AFFINE, BLK))
    )
    centre = (
        value(pair, 1, AFFINE + BLK, NRHS).astype(F32)
        + dot(middle, value(pair, 1, AFFINE, BLK))
        + dot(outflow, value(pair, 1, 2 * AFFINE, BLK))
    )
    inflow = jnp.where(core == 0, inflow, middle)
    outflow = jnp.where(core == 0, centre, outflow)
    flows = jnp.concatenate([inflow, outflow], axis=1).astype(BF16)
    for k in range(ROWS):
        response = jnp.concatenate([bwd[k, :BLK], bwd[k, AFFINE:]], axis=0)
        solved = bwd_values[k] + dot(flows, response)
        solution_ref[k] = solved
        rows[k] = solved.astype(BF16)

    rim_copies = [
        pltpu.make_async_remote_copy(
            src_ref=rows.at[pl.ds(ROWS - RIM, RIM)],
            dst_ref=rim.at[pl.ds(0, RIM)],
            send_sem=rim_send.at[0],
            recv_sem=rim_recv.at[0],
            device_id=part_up,
            device_id_type=MESH,
        ),
        pltpu.make_async_remote_copy(
            src_ref=rows.at[pl.ds(0, RIM)],
            dst_ref=rim.at[pl.ds(RIM, RIM)],
            send_sem=rim_send.at[1],
            recv_sem=rim_recv.at[1],
            device_id=part_down,
            device_id_type=MESH,
        ),
    ]
    for copy in rim_copies:
        copy.start()

    last_copy.wait_recv()
    edges_before = (inflow - dot(rows[0], last_in[...])) * has_before
    edges = pair_edges = jnp.stack([edges_before, outflow * has_after]).astype(BF16)
    rows[pl.ds(ROWS, 2)] = edges
    for copy in loads[4:]:
        copy.wait()
    totals = []
    for k in range(ROWS):
        lows = [rows[jnp.where(lower_index[k, m] == k, ROWS, lower_index[k, m])] for m in range(3)]
        highs = [
            rows[jnp.where(upper_index[k, m] == k, ROWS + 1, upper_index[k, m])] for m in range(3)
        ]
        total = dot(rows[k], diag[k])
        total = total + dot(jnp.concatenate(lows, axis=1), lower[k].reshape(3 * BLK, BLK))
        total = total + dot(jnp.concatenate(highs, axis=1), upper[k].reshape(3 * BLK, BLK))
        product_ref[k] = total

    for copy in rim_copies:
        copy.wait_recv()

    @pl.when(part == 0)
    def _():
        rim[pl.ds(0, RIM)] = jnp.zeros((RIM, NRHS, BLK), BF16)

    @pl.when(part == parts - 1)
    def _():
        rim[pl.ds(RIM, RIM)] = jnp.zeros((RIM, NRHS, BLK), BF16)

    for k in range(ROWS):
        sources = jnp.concatenate([rim[halo_index[k, h]] for h in range(2)], axis=1)
        product_ref[k] = product_ref[k] + dot(sources, halo[k].reshape(2 * BLK, BLK))

    pair_onward.wait_send()
    pair_back.wait_send()
    last_copy.wait_send()
    ends_copy.wait_send()
    for copy in rim_copies:
        copy.wait_send()
    for hop in range(right_hops):
        for piece in range(len(PIECES)):
            ring_copy(hop, piece).wait_send()

    @pl.when(core == 0)
    def _():
        for hop in range(right_hops, left_hops):
            for piece in range(len(PIECES)):
                ring_copy(hop, piece).wait_send()


def on_device(sections, parts, rhs, inverse, diag, lower, upper, halo, low_index, up_index, halo_index):
    chips = sections // 2
    hops = chips // 2
    smem = pl.BlockSpec(memory_space=pltpu.SMEM)
    hbm = pl.BlockSpec(memory_space=pl.ANY)
    vmem = pl.BlockSpec(memory_space=pltpu.VMEM)
    dma = pltpu.SemaphoreType.DMA
    return pl.pallas_call(
        functools.partial(kernel, sections, parts),
        out_shape=(
            jax.ShapeDtypeStruct(rhs.shape, F32),
            jax.ShapeDtypeStruct(rhs.shape, F32),
        ),
        in_specs=[smem] * 3 + [hbm] * 6,
        out_specs=(vmem, vmem),
        scratch_shapes=[
            pltpu.VMEM(rhs.shape, F32),
            pltpu.VMEM(inverse.shape, BF16),
            pltpu.VMEM(diag.shape, BF16),
            pltpu.VMEM(lower.shape, BF16),
            pltpu.VMEM(upper.shape, BF16),
            pltpu.VMEM(halo.shape, BF16),
            pltpu.VMEM((ROWS + 1, AFFINE, BLK), BF16),
            pltpu.VMEM((ROWS, AFFINE, BLK), F32),
            pltpu.VMEM((ROWS + 1, WIDE, BLK), BF16),
            pltpu.VMEM((ROWS, NRHS, BLK), F32),
            pltpu.VMEM((2, ELEMENT, BLK), BF16),
            pltpu.VMEM((hops + 2, ELEMENT, BLK), BF16),
            pltpu.VMEM((2, ELEMENT, BLK), BF16),
            pltpu.VMEM((BLK, BLK), BF16),
            pltpu.VMEM((BLK, BLK), BF16),
            pltpu.VMEM((ROWS + 2, NRHS, BLK), BF16),
            pltpu.VMEM((2 * RIM, NRHS, BLK), BF16),
            dma((6,)),
            dma((2,)),
            dma((2,)),
            dma((hops, len(PIECES))),
            dma((hops, len(PIECES))),
            dma((1,)),
            dma((1,)),
            dma((1,)),
            dma((1,)),
            dma((2,)),
            dma((2,)),
        ],
        compiler_params=pltpu.CompilerParams(collective_id=0, has_side_effects=True),
        name="block_ilu_apply",
    )(low_index, up_index, halo_index, rhs, inverse, diag, lower, upper, halo)


def solution(mesh):
    row = ("section", "dom")
    in_specs = (
        P(row, None, None),
        P(row, None, None),
        P(row, None, None),
        P(row, None, None, None),
        P(row, None, None, None),
        P(row, None, None, None),
        P(row, None),
        P(row, None),
        P(row, None),
    )
    out_specs = (P(row, None, None), P(row, None, None))
    body = functools.partial(on_device, mesh.shape["section"], mesh.shape["dom"])
    return jax.shard_map(
        body, mesh=mesh, in_specs=in_specs, out_specs=out_specs, check_vma=False
    )
```

```python
import functools

import jax
import jax.numpy as jnp
from jax import lax
from jax.experimental import pallas as pl
from jax.experimental.pallas import tpu as pltpu
from jax.sharding import PartitionSpec as P

F32 = jnp.float32
BF16 = jnp.bfloat16
MESH = pl.DeviceIdType.MESH
ROWS = 8
BLK = 128
NRHS = 32
RIM = 4
AFFINE = BLK + NRHS
WIDE = AFFINE + BLK
ELEMENT = AFFINE + WIDE
PIECES = ((0, AFFINE), (AFFINE, 2 * AFFINE), (2 * AFFINE, ELEMENT))


def dot(left, right):
    return jnp.dot(left.astype(BF16), right, preferred_element_type=F32)


def joined(left, right):
    right_m, right_a = right[:BLK], right[BLK:AFFINE]
    right_h, right_b = right[AFFINE : AFFINE + BLK], right[AFFINE + BLK : 2 * AFFINE]
    right_k, left_k = right[2 * AFFINE :], left[2 * AFFINE :]
    through = dot(left[:AFFINE], jnp.concatenate([right_m, right_h], axis=1))
    onward = jnp.concatenate(
        [through[:BLK, :BLK], through[BLK:, :BLK] + right_a.astype(F32)], axis=0
    )
    back = jnp.concatenate(
        [
            through[:BLK, BLK:].astype(BF16),
            (through[BLK:, BLK:] + right_b.astype(F32)).astype(BF16),
            right_k,
        ],
        axis=0,
    )
    back = dot(back, left_k)
    back = jnp.concatenate(
        [back[:AFFINE] + left[AFFINE : 2 * AFFINE].astype(F32), back[AFFINE:]], axis=0
    )
    return onward.astype(BF16), back.astype(BF16)


def kernel(
    sections,
    parts,
    lower_index,
    upper_index,
    halo_index,
    rhs_hbm,
    inverse_hbm,
    diag_hbm,
    lower_hbm,
    upper_hbm,
    halo_hbm,
    solution_ref,
    product_ref,
    rhs,
    inverse,
    diag,
    lower,
    upper,
    halo,
    fwd,
    fwd_wide,
    bwd,
    bwd_values,
    pair,
    ring,
    ends,
    last_own,
    last_in,
    rows,
    rim,
    load_sem,
    pair_send,
    pair_recv,
    ring_send,
    ring_recv,
    ends_send,
    ends_recv,
    last_send,
    last_recv,
    rim_send,
    rim_recv,
):
    chips = sections // 2
    left_hops = chips // 2
    right_hops = chips - 1 - left_hops
    section = lax.axis_index("section")
    part = lax.axis_index("dom")
    core = lax.rem(section, 2)
    chip = lax.div(section, 2)
    sibling = (section + 1 - 2 * core, part)
    onto = (2 * lax.rem(chip + 1 - 2 * core + chips, chips) + core, part)
    other = (2 * lax.rem(chip + 2 * core - 1 + chips, chips) + core, part)
    following = (lax.rem(section + 1, sections), part)
    beyond = (lax.rem(section + 2 * core - 1 + sections, sections), part)
    part_up = (section, lax.min(part + 1, parts - 1))
    part_down = (section, lax.max(part - 1, 0))

    loads = []
    for place, (source, target) in enumerate(
        (
            (lower_hbm, lower),
            (inverse_hbm, inverse),
            (rhs_hbm, rhs),
            (upper_hbm, upper),
            (diag_hbm, diag),
            (halo_hbm, halo),
        )
    ):
        copy = pltpu.make_async_copy(source, target, load_sem.at[place])
        copy.start()
        loads.append(copy)

    barrier = pltpu.get_barrier_semaphore()
    for device in (sibling, onto, other, beyond):
        pl.semaphore_signal(barrier, inc=1, device_id=device, device_id_type=MESH)

    @pl.when(part < parts - 1)
    def _():
        pl.semaphore_signal(barrier, inc=1, device_id=part_up, device_id_type=MESH)

    @pl.when(part > 0)
    def _():
        pl.semaphore_signal(barrier, inc=1, device_id=part_down, device_id_type=MESH)

    @pl.when(part == 0)
    def _():
        rim[pl.ds(0, RIM)] = jnp.zeros((RIM, NRHS, BLK), BF16)

    @pl.when(part == parts - 1)
    def _():
        rim[pl.ds(RIM, RIM)] = jnp.zeros((RIM, NRHS, BLK), BF16)

    spread = lax.broadcasted_iota(jnp.int32, (BLK, BLK), 0)
    identity = (spread == lax.broadcasted_iota(jnp.int32, (BLK, BLK), 1)).astype(F32)
    has_before = (section > 0).astype(F32)
    has_after = (section < sections - 1).astype(F32)
    fwd[ROWS, :BLK] = (identity * has_before).astype(BF16)
    fwd[ROWS, BLK:] = jnp.zeros((NRHS, BLK), BF16)
    bwd[ROWS, :AFFINE] = jnp.zeros((AFFINE, BLK), BF16)
    bwd[ROWS, AFFINE:] = (identity * has_after).astype(BF16)

    for copy in loads[:3]:
        copy.wait()
    for k in range(ROWS):
        folded = dot(lower[k].reshape(3 * BLK, BLK), inverse[k])
        base = jnp.concatenate([folded[:BLK] * -has_before, dot(rhs[k], inverse[k])], axis=0)
        slots = [jnp.where(lower_index[m, k] == k, ROWS, lower_index[m, k]) for m in (1, 2)]
        sources = jnp.concatenate([fwd[slot] for slot in slots], axis=1)
        wide = base - dot(sources, folded[BLK:].astype(BF16))
        fwd_wide[k] = wide
        fwd[k] = wide.astype(BF16)
    pair[core, :AFFINE] = fwd[ROWS - 1]

    partners = 4 + (part < parts - 1).astype(jnp.int32) + (part > 0).astype(jnp.int32)
    pl.semaphore_wait(barrier, partners)

    def pair_copy(piece, low, high):
        return pltpu.make_async_remote_copy(
            src_ref=pair.at[core, pl.ds(low, high - low)],
            dst_ref=pair.at[core, pl.ds(low, high - low)],
            send_sem=pair_send.at[piece],
            recv_sem=pair_recv.at[piece],
            device_id=sibling,
            device_id_type=MESH,
        )

    pair_onward = pair_copy(0, 0, AFFINE)
    pair_back = pair_copy(1, AFFINE, ELEMENT)
    pair_onward.start()

    loads[3].wait()
    for k in range(ROWS - 1, -1, -1):
        folded = dot(upper[k].reshape(3 * BLK, BLK), inverse[k])
        if k == ROWS - 1:
            last_own[...] = (folded[:BLK] + folded[BLK : 2 * BLK] + folded[2 * BLK :]).astype(BF16)
            last_copy = pltpu.make_async_remote_copy(
                src_ref=last_own,
                dst_ref=last_in,
                send_sem=last_send.at[0],
                recv_sem=last_recv.at[0],
                device_id=following,
                device_id_type=MESH,
            )
            last_copy.start()
        base = jnp.concatenate([fwd_wide[k], folded[:BLK] * -has_after], axis=0)
        slots = [jnp.where(upper_index[m, k] == k, ROWS, upper_index[m, k]) for m in (1, 2)]
        sources = jnp.concatenate([bwd[slot] for slot in slots], axis=1)
        wide = base - dot(sources, folded[BLK:].astype(BF16))
        bwd_values[k] = wide[BLK:AFFINE]
        bwd[k] = wide.astype(BF16)
    pair[core, AFFINE:] = bwd[0]
    pair_back.start()
    pair_onward.wait_recv()
    pair_back.wait_recv()
    onward, back = joined(pair[0], pair[1])
    ring[0, :AFFINE] = onward
    ring[0, AFFINE:] = back

    def ring_copy(hop, piece):
        low, high = PIECES[piece]
        return pltpu.make_async_remote_copy(
            src_ref=ring.at[hop, pl.ds(low, high - low)],
            dst_ref=ring.at[hop + 1, pl.ds(low, high - low)],
            send_sem=ring_send.at[hop, piece],
            recv_sem=ring_recv.at[hop, piece],
            device_id=onto,
            device_id_type=MESH,
        )

    for piece in range(len(PIECES)):
        ring_copy(0, piece).start()

    def take(hop, last):
        for piece in range(len(PIECES)):
            ring_copy(hop - 1, piece).wait_recv()
            if not last:
                ring_copy(hop, piece).start()

    def fold(hop, target, place):
        done = 1 if hop == 2 else left_hops + 1
        left = ring[jnp.where(core == 0, hop, done)]
        right = ring[jnp.where(core == 0, done, hop)]
        onward, back = joined(left, right)
        target[place, :AFFINE] = onward
        target[place, AFFINE:] = back

    for hop in range(1, right_hops):
        take(hop, False)
        if hop >= 2:
            fold(hop, ring, left_hops + 1)

    @pl.when(core == 0)
    def _():
        for hop in range(right_hops, left_hops + 1):
            take(hop, hop == left_hops)
            if hop == left_hops:
                fold(hop, ends, 0)
            elif hop >= 2:
                fold(hop, ring, left_hops + 1)

    @pl.when(core == 1)
    def _():
        take(right_hops, True)
        if right_hops >= 2:
            fold(right_hops, ends, 1)
        else:
            ends[1] = ring[1]

    ends_copy = pltpu.make_async_remote_copy(
        src_ref=ends.at[core],
        dst_ref=ends.at[core],
        send_sem=ends_send.at[0],
        recv_sem=ends_recv.at[0],
        device_id=sibling,
        device_id_type=MESH,
    )
    ends_copy.start()
    ends_copy.wait_recv()

    def value(ref, place, low, size):
        return ref[place, low : low + size]

    inflow = value(ends, 0, BLK, NRHS).astype(F32) + dot(
        value(ends, 1, BLK, NRHS), value(ends, 0, 0, BLK)
    )
    middle = value(pair, 0, BLK, NRHS).astype(F32) + dot(inflow, value(pair, 0, 0, BLK))
    outgoing = value(pair, 1, BLK, NRHS).astype(F32) + dot(middle, value(pair, 1, 0, BLK))
    far = value(ends, 1, BLK, NRHS).astype(F32) + dot(outgoing, value(ends, 1, 0, BLK))
    near = dot(outgoing, value(ends, 1, AFFINE, BLK))
    far = value(ends, 0, AFFINE + BLK, NRHS).astype(F32) + dot(far, value(ends, 0, AFFINE, BLK))
    outflow = (
        value(ends, 1, AFFINE + BLK, NRHS).astype(F32)
        + near
        + dot(far, value(ends, 1, 2 * AFFINE, BLK))
    )
    centre = (
        value(pair, 1, AFFINE + BLK, NRHS).astype(F32)
        + dot(middle, value(pair, 1, AFFINE, BLK))
        + dot(outflow, value(pair, 1, 2 * AFFINE, BLK))
    )
    inflow = jnp.where(core == 0, inflow, middle)
    outflow = jnp.where(core == 0, centre, outflow)
    flows = jnp.concatenate([inflow, outflow], axis=1).astype(BF16)
    for k in range(ROWS):
        response = jnp.concatenate([bwd[k, :BLK], bwd[k, AFFINE:]], axis=0)
        solved = bwd_values[k] + dot(flows, response)
        solution_ref[k] = solved
        rows[k] = solved.astype(BF16)

    rim_copies = [
        pltpu.make_async_remote_copy(
            src_ref=rows.at[pl.ds(ROWS - RIM, RIM)],
            dst_ref=rim.at[pl.ds(0, RIM)],
            send_sem=rim_send.at[0],
            recv_sem=rim_recv.at[0],
            device_id=part_up,
            device_id_type=MESH,
        ),
        pltpu.make_async_remote_copy(
            src_ref=rows.at[pl.ds(0, RIM)],
            dst_ref=rim.at[pl.ds(RIM, RIM)],
            send_sem=rim_send.at[1],
            recv_sem=rim_recv.at[1],
            device_id=part_down,
            device_id_type=MESH,
        ),
    ]
    @pl.when(part < parts - 1)
    def _():
        rim_copies[0].start()

    @pl.when(part > 0)
    def _():
        rim_copies[1].start()

    last_copy.wait_recv()
    edges_before = (inflow - dot(rows[0], last_in[...])) * has_before
    edges = jnp.stack([edges_before, outflow * has_after]).astype(BF16)
    rows[pl.ds(ROWS, 2)] = edges
    for copy in loads[4:]:
        copy.wait()
    totals = []
    for k in range(ROWS):
        lows = [rows[jnp.where(lower_index[m, k] == k, ROWS, lower_index[m, k])] for m in range(3)]
        highs = [
            rows[jnp.where(upper_index[m, k] == k, ROWS + 1, upper_index[m, k])] for m in range(3)
        ]
        total = dot(rows[k], diag[k])
        total = total + dot(jnp.concatenate(lows, axis=1), lower[k].reshape(3 * BLK, BLK))
        total = total + dot(jnp.concatenate(highs, axis=1), upper[k].reshape(3 * BLK, BLK))
        product_ref[k] = total

    @pl.when(part > 0)
    def _():
        rim_copies[0].wait_recv()

    @pl.when(part < parts - 1)
    def _():
        rim_copies[1].wait_recv()

    for k in range(ROWS):
        sources = jnp.concatenate([rim[halo_index[h, k]] for h in range(2)], axis=1)
        product_ref[k] = product_ref[k] + dot(sources, halo[k].reshape(2 * BLK, BLK))

    pair_onward.wait_send()
    pair_back.wait_send()
    last_copy.wait_send()
    ends_copy.wait_send()

    @pl.when(part < parts - 1)
    def _():
        rim_copies[0].wait_send()

    @pl.when(part > 0)
    def _():
        rim_copies[1].wait_send()

    for hop in range(right_hops):
        for piece in range(len(PIECES)):
            ring_copy(hop, piece).wait_send()

    @pl.when(core == 0)
    def _():
        for hop in range(right_hops, left_hops):
            for piece in range(len(PIECES)):
                ring_copy(hop, piece).wait_send()


def on_device(sections, parts, rhs, inverse, diag, lower, upper, halo, low_index, up_index, halo_index):
    chips = sections // 2
    hops = chips // 2
    smem = pl.BlockSpec(memory_space=pltpu.SMEM)
    hbm = pl.BlockSpec(memory_space=pl.ANY)
    vmem = pl.BlockSpec(memory_space=pltpu.VMEM)
    dma = pltpu.SemaphoreType.DMA
    return pl.pallas_call(
        functools.partial(kernel, sections, parts),
        out_shape=(
            pltpu.VMEM(rhs.shape, F32),
            pltpu.VMEM(rhs.shape, F32),
        ),
        in_specs=[smem] * 3 + [hbm] * 6,
        out_specs=(vmem, vmem),
        scratch_shapes=[
            pltpu.VMEM(rhs.shape, F32),
            pltpu.VMEM(inverse.shape, BF16),
            pltpu.VMEM(diag.shape, BF16),
            pltpu.VMEM(lower.shape, BF16),
            pltpu.VMEM(upper.shape, BF16),
            pltpu.VMEM(halo.shape, BF16),
            pltpu.VMEM((ROWS + 1, AFFINE, BLK), BF16),
            pltpu.VMEM((ROWS, AFFINE, BLK), F32),
            pltpu.VMEM((ROWS + 1, WIDE, BLK), BF16),
            pltpu.VMEM((ROWS, NRHS, BLK), F32),
            pltpu.VMEM((2, ELEMENT, BLK), BF16),
            pltpu.VMEM((hops + 2, ELEMENT, BLK), BF16),
            pltpu.VMEM((2, ELEMENT, BLK), BF16),
            pltpu.VMEM((BLK, BLK), BF16),
            pltpu.VMEM((BLK, BLK), BF16),
            pltpu.VMEM((ROWS + 2, NRHS, BLK), BF16),
            pltpu.VMEM((2 * RIM, NRHS, BLK), BF16),
            dma((6,)),
            dma((2,)),
            dma((2,)),
            dma((hops, len(PIECES))),
            dma((hops, len(PIECES))),
            dma((1,)),
            dma((1,)),
            dma((1,)),
            dma((1,)),
            dma((2,)),
            dma((2,)),
        ],
        compiler_params=pltpu.CompilerParams(collective_id=0, has_side_effects=True),
        name="block_ilu_apply",
    )(low_index.T, up_index.T, halo_index.T, rhs, inverse, diag, lower, upper, halo)


def solution(mesh):
    row = ("section", "dom")
    in_specs = (
        P(row, None, None),
        P(row, None, None),
        P(row, None, None),
        P(row, None, None, None),
        P(row, None, None, None),
        P(row, None, None, None),
        P(row, None),
        P(row, None),
        P(row, None),
    )
    out_specs = (P(row, None, None), P(row, None, None))
    body = functools.partial(on_device, mesh.shape["section"], mesh.shape["dom"])
    return jax.shard_map(
        body, mesh=mesh, in_specs=in_specs, out_specs=out_specs, check_vma=False
    )
```

```python
import functools

import jax
import jax.numpy as jnp
from jax import lax
from jax.experimental import pallas as pl
from jax.experimental.pallas import tpu as pltpu
from jax.sharding import PartitionSpec as P

F32 = jnp.float32
BF16 = jnp.bfloat16
MESH = pl.DeviceIdType.MESH
ROWS = 8
BLK = 128
NRHS = 32
RIM = 4
AFFINE = BLK + NRHS
WIDE = AFFINE + BLK
ELEMENT = AFFINE + WIDE
CHIPS = 8
FLOWS = (
    (4, 0, 0, 1),
    (4, 1, 0, 1),
    (-3, 1, 0, 0),
    (-3, 0, 0, 0),
    (3, 0, 0, 2),
    (3, 1, 0, 2),
    (-2, 1, 1, 1),
    (2, 0, 1, 0),
    (-1, 1, 1, 0),
    (1, 0, 1, 1),
)
PARTS_OF = ((0, AFFINE // 2), (AFFINE, WIDE // 2))


def dot(left, right):
    return jnp.dot(left.astype(BF16), right, preferred_element_type=F32)


def joined(left, right):
    right_m, right_a = right[:BLK], right[BLK:AFFINE]
    right_h, right_b = right[AFFINE : AFFINE + BLK], right[AFFINE + BLK : 2 * AFFINE]
    right_k, left_k = right[2 * AFFINE :], left[2 * AFFINE :]
    through = dot(left[:AFFINE], jnp.concatenate([right_m, right_h], axis=1))
    onward = jnp.concatenate(
        [through[:BLK, :BLK], through[BLK:, :BLK] + right_a.astype(F32)], axis=0
    )
    back = jnp.concatenate(
        [
            through[:BLK, BLK:].astype(BF16),
            (through[BLK:, BLK:] + right_b.astype(F32)).astype(BF16),
            right_k,
        ],
        axis=0,
    )
    back = dot(back, left_k)
    back = jnp.concatenate(
        [back[:AFFINE] + left[AFFINE : 2 * AFFINE].astype(F32), back[AFFINE:]], axis=0
    )
    return onward.astype(BF16), back.astype(BF16)


def kernel(
    sections,
    parts,
    lower_index,
    upper_index,
    halo_index,
    rhs_hbm,
    inverse_hbm,
    diag_hbm,
    lower_hbm,
    upper_hbm,
    halo_hbm,
    solution_ref,
    product_ref,
    rhs,
    inverse,
    diag,
    lower,
    upper,
    halo,
    fwd,
    fwd_wide,
    bwd,
    bwd_values,
    pair,
    whole,
    far,
    near,
    ends,
    last_own,
    last_in,
    rows,
    rim,
    load_sem,
    pair_send,
    pair_recv,
    flow_send,
    far_recv,
    near_recv,
    ends_send,
    ends_recv,
    last_send,
    last_recv,
    rim_send,
    rim_recv,
):
    section = lax.axis_index("section")
    part = lax.axis_index("dom")
    core = lax.rem(section, 2)
    chip = lax.div(section, 2)
    sibling = (section + 1 - 2 * core, part)
    following = (lax.rem(section + 1, sections), part)
    part_up = (section, lax.min(part + 1, parts - 1))
    part_down = (section, lax.max(part - 1, 0))

    loads = []
    for place, (source, target) in enumerate(
        (
            (lower_hbm, lower),
            (inverse_hbm, inverse),
            (rhs_hbm, rhs),
            (upper_hbm, upper),
            (diag_hbm, diag),
            (halo_hbm, halo),
        )
    ):
        copy = pltpu.make_async_copy(source, target, load_sem.at[place])
        copy.start()
        loads.append(copy)

    barrier = pltpu.get_barrier_semaphore()
    for step in range(1, sections):
        device = (lax.rem(section + step, sections), part)
        pl.semaphore_signal(barrier, inc=1, device_id=device, device_id_type=MESH)

    @pl.when(part < parts - 1)
    def _():
        pl.semaphore_signal(barrier, inc=1, device_id=part_up, device_id_type=MESH)

    @pl.when(part > 0)
    def _():
        pl.semaphore_signal(barrier, inc=1, device_id=part_down, device_id_type=MESH)

    @pl.when(part == 0)
    def _():
        rim[pl.ds(0, RIM)] = jnp.zeros((RIM, NRHS, BLK), BF16)

    @pl.when(part == parts - 1)
    def _():
        rim[pl.ds(RIM, RIM)] = jnp.zeros((RIM, NRHS, BLK), BF16)

    incoming = (
        (far, far_recv, 0, chip + 3 < CHIPS),
        (far, far_recv, 1, chip < 4),
        (far, far_recv, 2, chip < 3),
        (near, near_recv, 0, jnp.where(core == 0, chip < 2, chip + 1 < CHIPS)),
        (near, near_recv, 1, jnp.where(core == 0, chip < 1, chip + 2 < CHIPS)),
    )
    for buffer, _, slot, full in incoming:

        @pl.when(jnp.logical_not(full))
        def _(buffer=buffer, slot=slot):
            buffer[slot, AFFINE:] = jnp.zeros((WIDE, BLK), BF16)

    spread = lax.broadcasted_iota(jnp.int32, (BLK, BLK), 0)
    identity = (spread == lax.broadcasted_iota(jnp.int32, (BLK, BLK), 1)).astype(F32)
    has_before = (section > 0).astype(F32)
    has_after = (section < sections - 1).astype(F32)
    fwd[ROWS, :BLK] = (identity * has_before).astype(BF16)
    fwd[ROWS, BLK:] = jnp.zeros((NRHS, BLK), BF16)
    bwd[ROWS, :AFFINE] = jnp.zeros((AFFINE, BLK), BF16)
    bwd[ROWS, AFFINE:] = (identity * has_after).astype(BF16)

    for copy in loads[:3]:
        copy.wait()
    for k in range(ROWS):
        folded = dot(lower[k].reshape(3 * BLK, BLK), inverse[k])
        base = jnp.concatenate([folded[:BLK] * -has_before, dot(rhs[k], inverse[k])], axis=0)
        slots = [jnp.where(lower_index[m, k] == k, ROWS, lower_index[m, k]) for m in (1, 2)]
        sources = jnp.concatenate([fwd[slot] for slot in slots], axis=1)
        wide = base - dot(sources, folded[BLK:].astype(BF16))
        fwd_wide[k] = wide
        fwd[k] = wide.astype(BF16)
    pair[core, :AFFINE] = fwd[ROWS - 1]

    partners = sections - 1 + (part < parts - 1).astype(jnp.int32) + (part > 0).astype(jnp.int32)
    pl.semaphore_wait(barrier, partners)

    def pair_copy(piece, low, high):
        return pltpu.make_async_remote_copy(
            src_ref=pair.at[core, pl.ds(low, high - low)],
            dst_ref=pair.at[core, pl.ds(low, high - low)],
            send_sem=pair_send.at[piece],
            recv_sem=pair_recv.at[piece],
            device_id=sibling,
            device_id_type=MESH,
        )

    pair_onward = pair_copy(0, 0, AFFINE)
    pair_back = pair_copy(1, AFFINE, ELEMENT)
    pair_onward.start()

    loads[3].wait()
    for k in range(ROWS - 1, -1, -1):
        folded = dot(upper[k].reshape(3 * BLK, BLK), inverse[k])
        if k == ROWS - 1:
            last_own[...] = (folded[:BLK] + folded[BLK : 2 * BLK] + folded[2 * BLK :]).astype(BF16)
            last_copy = pltpu.make_async_remote_copy(
                src_ref=last_own,
                dst_ref=last_in,
                send_sem=last_send.at[0],
                recv_sem=last_recv.at[0],
                device_id=following,
                device_id_type=MESH,
            )
            last_copy.start()
        base = jnp.concatenate([fwd_wide[k], folded[:BLK] * -has_after], axis=0)
        slots = [jnp.where(upper_index[m, k] == k, ROWS, upper_index[m, k]) for m in (1, 2)]
        sources = jnp.concatenate([bwd[slot] for slot in slots], axis=1)
        wide = base - dot(sources, folded[BLK:].astype(BF16))
        bwd_values[k] = wide[BLK:AFFINE]
        bwd[k] = wide.astype(BF16)
    pair[core, AFFINE:] = bwd[0]
    pair_back.start()
    pair_onward.wait_recv()
    pair_back.wait_recv()
    onward, back = joined(pair[0], pair[1])
    whole[:AFFINE] = onward
    whole[AFFINE:] = back

    def flow_copy(index, kind):
        steps, target_core, buffer, slot = FLOWS[index]
        target = (2 * lax.rem(chip + steps + CHIPS, CHIPS) + target_core, part)
        low, size = PARTS_OF[kind]
        place = pl.ds(pl.multiple_of(low + size * core, 16), size)
        return pltpu.make_async_remote_copy(
            src_ref=whole.at[place],
            dst_ref=(far, near)[buffer].at[slot, place],
            send_sem=flow_send.at[index, kind],
            recv_sem=(far_recv, near_recv)[buffer].at[slot, core, kind],
            device_id=target,
            device_id_type=MESH,
        )

    def flow_full(index):
        steps = FLOWS[index][0]
        return chip + steps >= CHIPS if steps > 0 else chip + steps >= 0

    for index in range(len(FLOWS)):
        flow_copy(index, 0).start()
        pl.when(flow_full(index))(flow_copy(index, 1).start)

    def take(index):
        buffer, sems, slot, full = incoming[index]

        def landed(kind):
            low, size = PARTS_OF[kind]
            for half in range(2):
                place = pl.ds(low + size * half, size)
                pltpu.make_async_remote_copy(
                    src_ref=whole.at[place],
                    dst_ref=buffer.at[slot, place],
                    send_sem=flow_send.at[0, kind],
                    recv_sem=sems.at[slot, half, kind],
                    device_id=sibling,
                    device_id_type=MESH,
                ).wait_recv()

        landed(0)
        pl.when(full)(functools.partial(landed, 1))

    take(3)
    take(4)
    onward, back = joined(near[0], near[1])
    ends[core, :AFFINE] = onward
    ends[core, AFFINE:] = back
    ends_copy = pltpu.make_async_remote_copy(
        src_ref=ends.at[core],
        dst_ref=ends.at[core],
        send_sem=ends_send.at[0],
        recv_sem=ends_recv.at[0],
        device_id=sibling,
        device_id_type=MESH,
    )
    ends_copy.start()
    ends_copy.wait_recv()
    take(0)
    ahead = jnp.concatenate(joined(ends[1], far[0]), axis=0)
    take(2)
    behind = jnp.concatenate(joined(far[2], ends[0]), axis=0)
    take(1)
    behind = jnp.concatenate(joined(far[1], behind), axis=0)

    through = dot(
        ahead[:AFFINE], jnp.concatenate([behind[:BLK], behind[AFFINE : AFFINE + BLK]], axis=1)
    )
    inflow = through[BLK:, :BLK] + behind[BLK:AFFINE].astype(F32)
    back = jnp.concatenate(
        [
            through[:BLK, BLK:],
            through[BLK:, BLK:] + behind[AFFINE + BLK : 2 * AFFINE].astype(F32),
        ],
        axis=0,
    )
    back = dot(back, ahead[2 * AFFINE :]) + ahead[AFFINE : 2 * AFFINE].astype(F32)
    chip_maps = jnp.concatenate([whole[:BLK], pair[0, :BLK]], axis=1)
    passed = dot(inflow, chip_maps)
    outgoing = passed[:, :BLK] + whole[BLK:AFFINE].astype(F32)
    middle = passed[:, BLK:] + pair[0, BLK:AFFINE].astype(F32)
    outflow = back[BLK:] + dot(outgoing, back[:BLK].astype(BF16))
    centre = (
        pair[1, AFFINE + BLK : 2 * AFFINE].astype(F32)
        + dot(middle, pair[1, AFFINE : AFFINE + BLK])
        + dot(outflow, pair[1, 2 * AFFINE :])
    )
    inflow = jnp.where(core == 0, inflow, middle)
    outflow = jnp.where(core == 0, centre, outflow)
    flows = jnp.concatenate([inflow, outflow], axis=1).astype(BF16)
    for k in range(ROWS):
        response = jnp.concatenate([bwd[k, :BLK], bwd[k, AFFINE:]], axis=0)
        solved = bwd_values[k] + dot(flows, response)
        solution_ref[k] = solved
        rows[k] = solved.astype(BF16)

    rim_copies = [
        pltpu.make_async_remote_copy(
            src_ref=rows.at[pl.ds(ROWS - RIM, RIM)],
            dst_ref=rim.at[pl.ds(0, RIM)],
            send_sem=rim_send.at[0],
            recv_sem=rim_recv.at[0],
            device_id=part_up,
            device_id_type=MESH,
        ),
        pltpu.make_async_remote_copy(
            src_ref=rows.at[pl.ds(0, RIM)],
            dst_ref=rim.at[pl.ds(RIM, RIM)],
            send_sem=rim_send.at[1],
            recv_sem=rim_recv.at[1],
            device_id=part_down,
            device_id_type=MESH,
        ),
    ]
    @pl.when(part < parts - 1)
    def _():
        rim_copies[0].start()

    @pl.when(part > 0)
    def _():
        rim_copies[1].start()

    last_copy.wait_recv()
    edges_before = (inflow - dot(rows[0], last_in[...])) * has_before
    edges = jnp.stack([edges_before, outflow * has_after]).astype(BF16)
    rows[pl.ds(ROWS, 2)] = edges
    for copy in loads[4:]:
        copy.wait()
    totals = []
    for k in range(ROWS):
        lows = [rows[jnp.where(lower_index[m, k] == k, ROWS, lower_index[m, k])] for m in range(3)]
        highs = [
            rows[jnp.where(upper_index[m, k] == k, ROWS + 1, upper_index[m, k])] for m in range(3)
        ]
        total = dot(rows[k], diag[k])
        total = total + dot(jnp.concatenate(lows, axis=1), lower[k].reshape(3 * BLK, BLK))
        total = total + dot(jnp.concatenate(highs, axis=1), upper[k].reshape(3 * BLK, BLK))
        product_ref[k] = total

    @pl.when(part > 0)
    def _():
        rim_copies[0].wait_recv()

    @pl.when(part < parts - 1)
    def _():
        rim_copies[1].wait_recv()

    for k in range(ROWS):
        sources = jnp.concatenate([rim[halo_index[h, k]] for h in range(2)], axis=1)
        product_ref[k] = product_ref[k] + dot(sources, halo[k].reshape(2 * BLK, BLK))

    pair_onward.wait_send()
    pair_back.wait_send()
    last_copy.wait_send()
    ends_copy.wait_send()

    @pl.when(part < parts - 1)
    def _():
        rim_copies[0].wait_send()

    @pl.when(part > 0)
    def _():
        rim_copies[1].wait_send()

    for index in range(len(FLOWS)):
        flow_copy(index, 0).wait_send()
        pl.when(flow_full(index))(flow_copy(index, 1).wait_send)


def on_device(sections, parts, rhs, inverse, diag, lower, upper, halo, low_index, up_index, halo_index):
    smem = pl.BlockSpec(memory_space=pltpu.SMEM)
    hbm = pl.BlockSpec(memory_space=pl.ANY)
    vmem = pl.BlockSpec(memory_space=pltpu.VMEM)
    dma = pltpu.SemaphoreType.DMA
    return pl.pallas_call(
        functools.partial(kernel, sections, parts),
        out_shape=(
            pltpu.VMEM(rhs.shape, F32),
            pltpu.VMEM(rhs.shape, F32),
        ),
        in_specs=[smem] * 3 + [hbm] * 6,
        out_specs=(vmem, vmem),
        scratch_shapes=[
            pltpu.VMEM(rhs.shape, F32),
            pltpu.VMEM(inverse.shape, BF16),
            pltpu.VMEM(diag.shape, BF16),
            pltpu.VMEM(lower.shape, BF16),
            pltpu.VMEM(upper.shape, BF16),
            pltpu.VMEM(halo.shape, BF16),
            pltpu.VMEM((ROWS + 1, AFFINE, BLK), BF16),
            pltpu.VMEM((ROWS, AFFINE, BLK), F32),
            pltpu.VMEM((ROWS + 1, WIDE, BLK), BF16),
            pltpu.VMEM((ROWS, NRHS, BLK), F32),
            pltpu.VMEM((2, ELEMENT, BLK), BF16),
            pltpu.VMEM((ELEMENT, BLK), BF16),
            pltpu.VMEM((3, ELEMENT, BLK), BF16),
            pltpu.VMEM((2, ELEMENT, BLK), BF16),
            pltpu.VMEM((2, ELEMENT, BLK), BF16),
            pltpu.VMEM((BLK, BLK), BF16),
            pltpu.VMEM((BLK, BLK), BF16),
            pltpu.VMEM((ROWS + 2, NRHS, BLK), BF16),
            pltpu.VMEM((2 * RIM, NRHS, BLK), BF16),
            dma((6,)),
            dma((2,)),
            dma((2,)),
            dma((len(FLOWS), 2)),
            dma((3, 2, 2)),
            dma((2, 2, 2)),
            dma((1,)),
            dma((1,)),
            dma((1,)),
            dma((1,)),
            dma((2,)),
            dma((2,)),
        ],
        compiler_params=pltpu.CompilerParams(collective_id=0, has_side_effects=True),
        name="block_ilu_apply",
    )(low_index.T, up_index.T, halo_index.T, rhs, inverse, diag, lower, upper, halo)


def solution(mesh):
    row = ("section", "dom")
    in_specs = (
        P(row, None, None),
        P(row, None, None),
        P(row, None, None),
        P(row, None, None, None),
        P(row, None, None, None),
        P(row, None, None, None),
        P(row, None),
        P(row, None),
        P(row, None),
    )
    out_specs = (P(row, None, None), P(row, None, None))
    body = functools.partial(on_device, mesh.shape["section"], mesh.shape["dom"])
    return jax.shard_map(
        body, mesh=mesh, in_specs=in_specs, out_specs=out_specs, check_vma=False
    )
```

```python
import functools

import jax
import jax.numpy as jnp
from jax import lax
from jax.experimental import pallas as pl
from jax.experimental.pallas import tpu as pltpu
from jax.sharding import PartitionSpec as P

F32 = jnp.float32
BF16 = jnp.bfloat16
MESH = pl.DeviceIdType.MESH
ROWS = 8
BLK = 128
NRHS = 32
RIM = 4
AFFINE = BLK + NRHS
WIDE = AFFINE + BLK
ELEMENT = AFFINE + WIDE


def dot(left, right):
    return jnp.dot(left.astype(BF16), right, preferred_element_type=F32)


def joined(left, right):
    right_m, right_a = right[:BLK], right[BLK:AFFINE]
    right_h, right_b = right[AFFINE : AFFINE + BLK], right[AFFINE + BLK : 2 * AFFINE]
    right_k, left_k = right[2 * AFFINE :], left[2 * AFFINE :]
    through = dot(left[:AFFINE], jnp.concatenate([right_m, right_h], axis=1))
    onward = jnp.concatenate(
        [through[:BLK, :BLK], through[BLK:, :BLK] + right_a.astype(F32)], axis=0
    )
    back = jnp.concatenate(
        [
            through[:BLK, BLK:].astype(BF16),
            (through[BLK:, BLK:] + right_b.astype(F32)).astype(BF16),
            right_k,
        ],
        axis=0,
    )
    back = dot(back, left_k)
    back = jnp.concatenate(
        [back[:AFFINE] + left[AFFINE : 2 * AFFINE].astype(F32), back[AFFINE:]], axis=0
    )
    return onward.astype(BF16), back.astype(BF16)


def kernel(
    sections,
    parts,
    lower_index,
    upper_index,
    halo_index,
    rhs_hbm,
    inverse_hbm,
    diag_hbm,
    lower_hbm,
    upper_hbm,
    halo_hbm,
    solution_ref,
    product_ref,
    rhs,
    inverse,
    diag,
    lower,
    upper,
    halo,
    fwd,
    fwd_wide,
    bwd,
    bwd_values,
    pair,
    whole,
    elements,
    inflows,
    outflows,
    got,
    last_own,
    last_in,
    rows,
    rim,
    load_sem,
    pair_send,
    pair_recv,
    element_send,
    element_recv,
    result_send,
    got_recv,
    last_send,
    last_recv,
    rim_send,
    rim_recv,
):
    chips = sections // 2
    hub = chips // 2
    section = lax.axis_index("section")
    part = lax.axis_index("dom")
    core = lax.rem(section, 2)
    chip = lax.div(section, 2)
    sibling = (section + 1 - 2 * core, part)
    at_hub = section == 2 * hub
    hub_device = (2 * hub, part)
    beyond = (lax.rem(section + 2 * core - 1 + sections, sections), part)
    following = (lax.rem(section + 1, sections), part)
    part_up = (section, lax.min(part + 1, parts - 1))
    part_down = (section, lax.max(part - 1, 0))

    loads = []
    for place, (source, target) in enumerate(
        (
            (lower_hbm, lower),
            (inverse_hbm, inverse),
            (rhs_hbm, rhs),
            (upper_hbm, upper),
            (diag_hbm, diag),
            (halo_hbm, halo),
        )
    ):
        copy = pltpu.make_async_copy(source, target, load_sem.at[place])
        copy.start()
        loads.append(copy)

    barrier = pltpu.get_barrier_semaphore()
    for device in (sibling, beyond):
        pl.semaphore_signal(barrier, inc=1, device_id=device, device_id_type=MESH)

    @pl.when(at_hub)
    def _():
        for other in range(sections):
            if other != 2 * hub:
                pl.semaphore_signal(barrier, inc=1, device_id=(other, part), device_id_type=MESH)

    @pl.when(jnp.logical_not(at_hub))
    def _():
        pl.semaphore_signal(barrier, inc=1, device_id=hub_device, device_id_type=MESH)

    @pl.when(part < parts - 1)
    def _():
        pl.semaphore_signal(barrier, inc=1, device_id=part_up, device_id_type=MESH)

    @pl.when(part > 0)
    def _():
        pl.semaphore_signal(barrier, inc=1, device_id=part_down, device_id_type=MESH)

    @pl.when(part == 0)
    def _():
        rim[pl.ds(0, RIM)] = jnp.zeros((RIM, NRHS, BLK), BF16)

    @pl.when(part == parts - 1)
    def _():
        rim[pl.ds(RIM, RIM)] = jnp.zeros((RIM, NRHS, BLK), BF16)

    @pl.when(chip == 0)
    def _():
        got[0] = jnp.zeros((NRHS, BLK), BF16)

    @pl.when(chip == chips - 1)
    def _():
        got[1] = jnp.zeros((NRHS, BLK), BF16)

    spread = lax.broadcasted_iota(jnp.int32, (BLK, BLK), 0)
    identity = (spread == lax.broadcasted_iota(jnp.int32, (BLK, BLK), 1)).astype(F32)
    has_before = (section > 0).astype(F32)
    has_after = (section < sections - 1).astype(F32)
    fwd[ROWS, :BLK] = (identity * has_before).astype(BF16)
    fwd[ROWS, BLK:] = jnp.zeros((NRHS, BLK), BF16)
    bwd[ROWS, :AFFINE] = jnp.zeros((AFFINE, BLK), BF16)
    bwd[ROWS, AFFINE:] = (identity * has_after).astype(BF16)

    for copy in loads[:3]:
        copy.wait()
    for k in range(ROWS):
        folded = dot(lower[k].reshape(3 * BLK, BLK), inverse[k])
        base = jnp.concatenate([folded[:BLK] * -has_before, dot(rhs[k], inverse[k])], axis=0)
        slots = [jnp.where(lower_index[m, k] == k, ROWS, lower_index[m, k]) for m in (1, 2)]
        sources = jnp.concatenate([fwd[slot] for slot in slots], axis=1)
        wide = base - dot(sources, folded[BLK:].astype(BF16))
        fwd_wide[k] = wide
        fwd[k] = wide.astype(BF16)
    pair[core, :AFFINE] = fwd[ROWS - 1]

    partners = jnp.where(at_hub, sections + 1, 3) + (part < parts - 1).astype(jnp.int32) + (part > 0).astype(jnp.int32)
    pl.semaphore_wait(barrier, partners)

    def pair_copy(piece, low, high):
        return pltpu.make_async_remote_copy(
            src_ref=pair.at[core, pl.ds(low, high - low)],
            dst_ref=pair.at[core, pl.ds(low, high - low)],
            send_sem=pair_send.at[piece],
            recv_sem=pair_recv.at[piece],
            device_id=sibling,
            device_id_type=MESH,
        )

    pair_onward = pair_copy(0, 0, AFFINE)
    pair_back = pair_copy(1, AFFINE, ELEMENT)
    pair_onward.start()

    loads[3].wait()
    for k in range(ROWS - 1, -1, -1):
        folded = dot(upper[k].reshape(3 * BLK, BLK), inverse[k])
        if k == ROWS - 1:
            last_own[...] = (folded[:BLK] + folded[BLK : 2 * BLK] + folded[2 * BLK :]).astype(BF16)
            last_copy = pltpu.make_async_remote_copy(
                src_ref=last_own,
                dst_ref=last_in,
                send_sem=last_send.at[0],
                recv_sem=last_recv.at[0],
                device_id=following,
                device_id_type=MESH,
            )
            last_copy.start()
        base = jnp.concatenate([fwd_wide[k], folded[:BLK] * -has_after], axis=0)
        slots = [jnp.where(upper_index[m, k] == k, ROWS, upper_index[m, k]) for m in (1, 2)]
        sources = jnp.concatenate([bwd[slot] for slot in slots], axis=1)
        wide = base - dot(sources, folded[BLK:].astype(BF16))
        bwd_values[k] = wide[BLK:AFFINE]
        bwd[k] = wide.astype(BF16)
    pair[core, AFFINE:] = bwd[0]
    pair_back.start()
    pair_onward.wait_recv()
    pair_back.wait_recv()
    onward, back = joined(pair[0], pair[1])
    whole[:AFFINE] = onward
    whole[AFFINE:] = back

    def element_copy(origin, half, low, rows_sent):
        place = pl.ds(pl.multiple_of(low + rows_sent * half, 16), rows_sent)
        return pltpu.make_async_remote_copy(
            src_ref=whole.at[place],
            dst_ref=elements.at[origin, place],
            send_sem=element_send.at[0],
            recv_sem=element_recv.at[origin, half],
            device_id=hub_device,
            device_id_type=MESH,
        )

    def extent(origin):
        if origin == 0:
            return BLK, NRHS // 2
        if origin == chips - 1:
            return AFFINE, AFFINE // 2
        return 0, ELEMENT // 2

    groups = (
        (chip == 0, 0),
        (chip == chips - 1, chips - 1),
        ((chip > 0) & (chip < chips - 1) & (chip != hub), 1),
    )
    for member, kind in groups:

        @pl.when(member)
        def _(kind=kind):
            element_copy(chip, core, *extent(kind)).start()

    def result_copy(kind, target, target_core):
        return pltpu.make_async_remote_copy(
            src_ref=(inflows, outflows)[kind].at[target],
            dst_ref=got.at[kind],
            send_sem=result_send.at[target, kind, target_core],
            recv_sem=got_recv.at[kind],
            device_id=(2 * target + target_core, part),
            device_id_type=MESH,
        )

    def result_copies(kind, target):
        return [
            result_copy(kind, target, target_core)
            for target_core in (1, 0)
            if (target, target_core) != (hub, 0)
        ]

    @pl.when(at_hub)
    def _():
        def take(origin):
            for half in range(2):
                element_copy(origin, half, *extent(origin)).wait_recv()

        def part_of(origin, low, size):
            ref = whole if origin == hub else elements.at[origin]
            return ref[low : low + size]

        running = None
        for origin in range(chips):
            if origin > 0:
                inflows[origin] = running.astype(BF16)
                for copy in result_copies(0, origin):
                    copy.start()
            if origin != hub:
                take(origin)
            if origin < chips - 1:
                values = part_of(origin, BLK, NRHS).astype(F32)
                if origin > 0:
                    values = values + dot(running, part_of(origin, 0, BLK))
                running = values
        running = None
        for origin in range(chips - 1, 0, -1):
            values = part_of(origin, AFFINE + BLK, NRHS).astype(F32)
            values = values + dot(inflows[origin], part_of(origin, AFFINE, BLK))
            if origin < chips - 1:
                values = values + dot(running, part_of(origin, 2 * AFFINE, BLK))
            running = values
            outflows[origin - 1] = running.astype(BF16)
        for target in range(chips - 1):
            target = (target + 1) // 2 if target % 2 == 0 else chips - 1 - (target + 1) // 2
            for copy in result_copies(1, target):
                copy.start()
        got[0] = inflows[hub]
        got[1] = outflows[hub]

    @pl.when(jnp.logical_not(at_hub) & (chip > 0))
    def _():
        result_copy(0, 1, 0).wait_recv()

    inflow = got[0].astype(F32)
    middle = dot(inflow, pair[0, :BLK]) + pair[0, BLK:AFFINE].astype(F32)
    centre = pair[1, AFFINE + BLK : 2 * AFFINE].astype(F32) + dot(
        middle, pair[1, AFFINE : AFFINE + BLK]
    )

    @pl.when(jnp.logical_not(at_hub) & (chip < chips - 1))
    def _():
        result_copy(1, 1, 0).wait_recv()

    outflow = got[1].astype(F32)
    centre = centre + dot(got[1], pair[1, 2 * AFFINE :])
    inflow = jnp.where(core == 0, inflow, middle)
    outflow = jnp.where(core == 0, centre, outflow)
    flows = jnp.concatenate([inflow, outflow], axis=1).astype(BF16)
    for k in range(ROWS):
        response = jnp.concatenate([bwd[k, :BLK], bwd[k, AFFINE:]], axis=0)
        solved = bwd_values[k] + dot(flows, response)
        solution_ref[k] = solved
        rows[k] = solved.astype(BF16)

    rim_copies = [
        pltpu.make_async_remote_copy(
            src_ref=rows.at[pl.ds(ROWS - RIM, RIM)],
            dst_ref=rim.at[pl.ds(0, RIM)],
            send_sem=rim_send.at[0],
            recv_sem=rim_recv.at[0],
            device_id=part_up,
            device_id_type=MESH,
        ),
        pltpu.make_async_remote_copy(
            src_ref=rows.at[pl.ds(0, RIM)],
            dst_ref=rim.at[pl.ds(RIM, RIM)],
            send_sem=rim_send.at[1],
            recv_sem=rim_recv.at[1],
            device_id=part_down,
            device_id_type=MESH,
        ),
    ]
    @pl.when(part < parts - 1)
    def _():
        rim_copies[0].start()

    @pl.when(part > 0)
    def _():
        rim_copies[1].start()

    last_copy.wait_recv()
    edges_before = (inflow - dot(rows[0], last_in[...])) * has_before
    edges = jnp.stack([edges_before, outflow * has_after]).astype(BF16)
    rows[pl.ds(ROWS, 2)] = edges
    for copy in loads[4:]:
        copy.wait()
    totals = []
    for k in range(ROWS):
        lows = [rows[jnp.where(lower_index[m, k] == k, ROWS, lower_index[m, k])] for m in range(3)]
        highs = [
            rows[jnp.where(upper_index[m, k] == k, ROWS + 1, upper_index[m, k])] for m in range(3)
        ]
        total = dot(rows[k], diag[k])
        total = total + dot(jnp.concatenate(lows, axis=1), lower[k].reshape(3 * BLK, BLK))
        total = total + dot(jnp.concatenate(highs, axis=1), upper[k].reshape(3 * BLK, BLK))
        product_ref[k] = total

    @pl.when(part > 0)
    def _():
        rim_copies[0].wait_recv()

    @pl.when(part < parts - 1)
    def _():
        rim_copies[1].wait_recv()

    for k in range(ROWS):
        sources = jnp.concatenate([rim[halo_index[h, k]] for h in range(2)], axis=1)
        product_ref[k] = product_ref[k] + dot(sources, halo[k].reshape(2 * BLK, BLK))

    pair_onward.wait_send()
    pair_back.wait_send()
    last_copy.wait_send()

    @pl.when(part < parts - 1)
    def _():
        rim_copies[0].wait_send()

    @pl.when(part > 0)
    def _():
        rim_copies[1].wait_send()

    for member, kind in groups:

        @pl.when(member)
        def _(kind=kind):
            element_copy(chip, core, *extent(kind)).wait_send()

    @pl.when(at_hub)
    def _():
        for kind in range(2):
            for target in range(1 - kind, chips - kind):
                for copy in result_copies(kind, target):
                    copy.wait_send()


def on_device(sections, parts, rhs, inverse, diag, lower, upper, halo, low_index, up_index, halo_index):
    chips = sections // 2
    smem = pl.BlockSpec(memory_space=pltpu.SMEM)
    hbm = pl.BlockSpec(memory_space=pl.ANY)
    vmem = pl.BlockSpec(memory_space=pltpu.VMEM)
    dma = pltpu.SemaphoreType.DMA
    return pl.pallas_call(
        functools.partial(kernel, sections, parts),
        out_shape=(
            pltpu.VMEM(rhs.shape, F32),
            pltpu.VMEM(rhs.shape, F32),
        ),
        in_specs=[smem] * 3 + [hbm] * 6,
        out_specs=(vmem, vmem),
        scratch_shapes=[
            pltpu.VMEM(rhs.shape, F32),
            pltpu.VMEM(inverse.shape, BF16),
            pltpu.VMEM(diag.shape, BF16),
            pltpu.VMEM(lower.shape, BF16),
            pltpu.VMEM(upper.shape, BF16),
            pltpu.VMEM(halo.shape, BF16),
            pltpu.VMEM((ROWS + 1, AFFINE, BLK), BF16),
            pltpu.VMEM((ROWS, AFFINE, BLK), F32),
            pltpu.VMEM((ROWS + 1, WIDE, BLK), BF16),
            pltpu.VMEM((ROWS, NRHS, BLK), F32),
            pltpu.VMEM((2, ELEMENT, BLK), BF16),
            pltpu.VMEM((ELEMENT, BLK), BF16),
            pltpu.VMEM((chips, ELEMENT, BLK), BF16),
            pltpu.VMEM((chips, NRHS, BLK), BF16),
            pltpu.VMEM((chips, NRHS, BLK), BF16),
            pltpu.VMEM((2, NRHS, BLK), BF16),
            pltpu.VMEM((BLK, BLK), BF16),
            pltpu.VMEM((BLK, BLK), BF16),
            pltpu.VMEM((ROWS + 2, NRHS, BLK), BF16),
            pltpu.VMEM((2 * RIM, NRHS, BLK), BF16),
            dma((6,)),
            dma((2,)),
            dma((2,)),
            dma((1,)),
            dma((chips, 2)),
            dma((chips, 2, 2)),
            dma((2,)),
            dma((1,)),
            dma((1,)),
            dma((2,)),
            dma((2,)),
        ],
        compiler_params=pltpu.CompilerParams(collective_id=0, has_side_effects=True),
        name="block_ilu_apply",
    )(low_index.T, up_index.T, halo_index.T, rhs, inverse, diag, lower, upper, halo)


def solution(mesh):
    row = ("section", "dom")
    in_specs = (
        P(row, None, None),
        P(row, None, None),
        P(row, None, None),
        P(row, None, None, None),
        P(row, None, None, None),
        P(row, None, None, None),
        P(row, None),
        P(row, None),
        P(row, None),
    )
    out_specs = (P(row, None, None), P(row, None, None))
    body = functools.partial(on_device, mesh.shape["section"], mesh.shape["dom"])
    return jax.shard_map(
        body, mesh=mesh, in_specs=in_specs, out_specs=out_specs, check_vma=False
    )
```

```python
import functools

import jax
import jax.numpy as jnp
from jax import lax
from jax.experimental import pallas as pl
from jax.experimental.pallas import tpu as pltpu
from jax.sharding import PartitionSpec as P

F32 = jnp.float32
BF16 = jnp.bfloat16
MESH = pl.DeviceIdType.MESH
ROWS = 8
BLK = 128
NRHS = 32
RIM = 4
AFFINE = BLK + NRHS
WIDE = AFFINE + BLK
ELEMENT = AFFINE + WIDE


def dot(left, right):
    return jnp.dot(left.astype(BF16), right, preferred_element_type=F32)


def joined(left, right):
    right_m, right_a = right[:BLK], right[BLK:AFFINE]
    right_h, right_b = right[AFFINE : AFFINE + BLK], right[AFFINE + BLK : 2 * AFFINE]
    right_k, left_k = right[2 * AFFINE :], left[2 * AFFINE :]
    through = dot(left[:AFFINE], jnp.concatenate([right_m, right_h], axis=1))
    onward = jnp.concatenate(
        [through[:BLK, :BLK], through[BLK:, :BLK] + right_a.astype(F32)], axis=0
    )
    back = jnp.concatenate(
        [
            through[:BLK, BLK:].astype(BF16),
            (through[BLK:, BLK:] + right_b.astype(F32)).astype(BF16),
            right_k,
        ],
        axis=0,
    )
    back = dot(back, left_k)
    back = jnp.concatenate(
        [back[:AFFINE] + left[AFFINE : 2 * AFFINE].astype(F32), back[AFFINE:]], axis=0
    )
    return onward.astype(BF16), back.astype(BF16)


def kernel(
    sections,
    parts,
    lower_index_hbm,
    upper_index_hbm,
    halo_index_hbm,
    rhs_hbm,
    inverse_hbm,
    diag_hbm,
    lower_hbm,
    upper_hbm,
    halo_hbm,
    solution_ref,
    product_ref,
    lower_index,
    upper_index,
    halo_index,
    rhs,
    inverse,
    diag,
    lower,
    upper,
    halo,
    fwd,
    fwd_wide,
    bwd,
    bwd_values,
    pair,
    whole,
    elements,
    inflows,
    outflows,
    got,
    last_own,
    last_in,
    rows,
    rim,
    load_sem,
    pair_send,
    pair_recv,
    element_send,
    element_recv,
    result_send,
    got_recv,
    last_send,
    last_recv,
    rim_send,
    rim_recv,
):
    chips = sections // 2
    middle_chip = chips // 2
    section = lax.axis_index("section")
    part = lax.axis_index("dom")
    core = lax.rem(section, 2)
    chip = lax.div(section, 2)
    sibling = (section + 1 - 2 * core, part)
    at_hub = section == 1
    hub_device = (1, part)
    beyond = (lax.rem(section + 2 * core - 1 + sections, sections), part)
    following = (lax.rem(section + 1, sections), part)
    part_up = (section, lax.min(part + 1, parts - 1))
    part_down = (section, lax.max(part - 1, 0))

    loads = []
    for place, (source, target) in enumerate(
        (
            (lower_index_hbm, lower_index),
            (lower_hbm, lower),
            (inverse_hbm, inverse),
            (rhs_hbm, rhs),
            (upper_index_hbm, upper_index),
            (upper_hbm, upper),
            (halo_index_hbm, halo_index),
            (diag_hbm, diag),
            (halo_hbm, halo),
        )
    ):
        copy = pltpu.make_async_copy(source, target, load_sem.at[place])
        copy.start()
        loads.append(copy)

    barrier = pltpu.get_barrier_semaphore()
    for device in (sibling, beyond):
        pl.semaphore_signal(barrier, inc=1, device_id=device, device_id_type=MESH)

    @pl.when(at_hub)
    def _():
        for other in range(sections):
            if other != 1:
                pl.semaphore_signal(barrier, inc=1, device_id=(other, part), device_id_type=MESH)

    @pl.when(jnp.logical_not(at_hub))
    def _():
        pl.semaphore_signal(barrier, inc=1, device_id=hub_device, device_id_type=MESH)

    @pl.when(part < parts - 1)
    def _():
        pl.semaphore_signal(barrier, inc=1, device_id=part_up, device_id_type=MESH)

    @pl.when(part > 0)
    def _():
        pl.semaphore_signal(barrier, inc=1, device_id=part_down, device_id_type=MESH)

    @pl.when(part == 0)
    def _():
        rim[pl.ds(0, RIM)] = jnp.zeros((RIM, NRHS, BLK), BF16)

    @pl.when(part == parts - 1)
    def _():
        rim[pl.ds(RIM, RIM)] = jnp.zeros((RIM, NRHS, BLK), BF16)

    @pl.when(chip == 0)
    def _():
        got[0] = jnp.zeros((NRHS, BLK), BF16)

    @pl.when(chip == chips - 1)
    def _():
        got[1] = jnp.zeros((NRHS, BLK), BF16)

    spread = lax.broadcasted_iota(jnp.int32, (BLK, BLK), 0)
    identity = (spread == lax.broadcasted_iota(jnp.int32, (BLK, BLK), 1)).astype(F32)
    has_before = (section > 0).astype(F32)
    has_after = (section < sections - 1).astype(F32)
    fwd[ROWS, :BLK] = (identity * has_before).astype(BF16)
    fwd[ROWS, BLK:] = jnp.zeros((NRHS, BLK), BF16)
    bwd[ROWS, :AFFINE] = jnp.zeros((AFFINE, BLK), BF16)
    bwd[ROWS, AFFINE:] = (identity * has_after).astype(BF16)

    for copy in loads[:4]:
        copy.wait()
    for k in range(ROWS):
        folded = dot(lower[k].reshape(3 * BLK, BLK), inverse[k])
        base = jnp.concatenate([folded[:BLK] * -has_before, dot(rhs[k], inverse[k])], axis=0)
        slots = [jnp.where(lower_index[m, k] == k, ROWS, lower_index[m, k]) for m in (1, 2)]
        sources = jnp.concatenate([fwd[slot] for slot in slots], axis=1)
        wide = base - dot(sources, folded[BLK:].astype(BF16))
        fwd_wide[k] = wide
        fwd[k] = wide.astype(BF16)
    pair[core, :AFFINE] = fwd[ROWS - 1]

    partners = jnp.where(at_hub, sections + 1, 3) + (part < parts - 1).astype(jnp.int32) + (part > 0).astype(jnp.int32)
    pl.semaphore_wait(barrier, partners)

    def pair_copy(piece, low, high):
        return pltpu.make_async_remote_copy(
            src_ref=pair.at[core, pl.ds(low, high - low)],
            dst_ref=pair.at[core, pl.ds(low, high - low)],
            send_sem=pair_send.at[piece],
            recv_sem=pair_recv.at[piece],
            device_id=sibling,
            device_id_type=MESH,
        )

    pair_onward = pair_copy(0, 0, AFFINE)
    pair_back = pair_copy(1, AFFINE, ELEMENT)
    pair_onward.start()

    for copy in loads[4:6]:
        copy.wait()
    for k in range(ROWS - 1, -1, -1):
        folded = dot(upper[k].reshape(3 * BLK, BLK), inverse[k])
        if k == ROWS - 1:
            last_own[...] = (folded[:BLK] + folded[BLK : 2 * BLK] + folded[2 * BLK :]).astype(BF16)
            last_copy = pltpu.make_async_remote_copy(
                src_ref=last_own,
                dst_ref=last_in,
                send_sem=last_send.at[0],
                recv_sem=last_recv.at[0],
                device_id=following,
                device_id_type=MESH,
            )
            last_copy.start()
        base = jnp.concatenate([fwd_wide[k], folded[:BLK] * -has_after], axis=0)
        slots = [jnp.where(upper_index[m, k] == k, ROWS, upper_index[m, k]) for m in (1, 2)]
        sources = jnp.concatenate([bwd[slot] for slot in slots], axis=1)
        wide = base - dot(sources, folded[BLK:].astype(BF16))
        bwd_values[k] = wide[BLK:AFFINE]
        bwd[k] = wide.astype(BF16)
    pair[core, AFFINE:] = bwd[0]
    pair_back.start()
    pair_onward.wait_recv()
    pair_back.wait_recv()
    onward, back = joined(pair[0], pair[1])
    whole[:AFFINE] = onward
    whole[AFFINE:] = back

    def element_copy(origin, half, low, rows_sent):
        place = pl.ds(pl.multiple_of(low + rows_sent * half, 16), rows_sent)
        return pltpu.make_async_remote_copy(
            src_ref=whole.at[place],
            dst_ref=elements.at[origin, place],
            send_sem=element_send.at[0],
            recv_sem=element_recv.at[origin, half],
            device_id=hub_device,
            device_id_type=MESH,
        )

    def extent(origin):
        return (AFFINE, AFFINE // 2) if origin == chips - 1 else (0, ELEMENT // 2)

    groups = (
        (chip == chips - 1, chips - 1),
        ((chip > 0) & (chip < chips - 1), 1),
    )
    for member, kind in groups:

        @pl.when(member)
        def _(kind=kind):
            element_copy(chip, core, *extent(kind)).start()

    def result_copy(kind, target, target_core):
        return pltpu.make_async_remote_copy(
            src_ref=(inflows, outflows)[kind].at[target],
            dst_ref=got.at[kind],
            send_sem=result_send.at[target, kind, target_core],
            recv_sem=got_recv.at[kind],
            device_id=(2 * target + target_core, part),
            device_id_type=MESH,
        )

    def result_copies(kind, target):
        return [
            result_copy(kind, target, target_core)
            for target_core in (0, 1)
            if (target, target_core) != (0, 1)
        ]

    @pl.when(at_hub)
    def _():
        def take(origin):
            for half in range(2):
                element_copy(origin, half, *extent(origin)).wait_recv()

        def part_of(origin, low, size):
            ref = elements.at[origin] if origin else whole
            return ref[low : low + size]

        def onward(origin, running):
            values = part_of(origin, BLK, NRHS).astype(F32)
            return values + dot(running, part_of(origin, 0, BLK)) if origin else values

        def give(kind, target, values):
            (inflows, outflows)[kind][target] = values.astype(BF16)
            for copy in result_copies(kind, target):
                copy.start()

        for origin in sorted(range(1, chips), key=lambda c: min(c, chips - c)):
            if origin != middle_chip:
                take(origin)
        running = None
        known = [None] * chips
        for origin in range(middle_chip):
            running = onward(origin, running)
            give(0, origin + 1, running)
            if origin:
                known[origin] = part_of(origin, AFFINE + BLK, NRHS).astype(F32) + dot(
                    inflows[origin], part_of(origin, AFFINE, BLK)
                )
        runs = [None] * chips
        runs[-1] = part_of(chips - 1, AFFINE, AFFINE)
        for origin in range(chips - 2, middle_chip, -1):
            spread_b = jnp.concatenate(
                [jnp.zeros((BLK, BLK), F32), runs[origin + 1][BLK:].astype(F32)], axis=0
            )
            through = dot(part_of(origin, 0, AFFINE), runs[origin + 1][:BLK]) + spread_b
            through = dot(through, part_of(origin, 2 * AFFINE, BLK))
            runs[origin] = (through + part_of(origin, AFFINE, AFFINE).astype(F32)).astype(BF16)
        take(middle_chip)
        known[middle_chip] = part_of(middle_chip, AFFINE + BLK, NRHS).astype(F32) + dot(
            inflows[middle_chip], part_of(middle_chip, AFFINE, BLK)
        )

        def returned(origin, running):
            return runs[origin + 1][BLK:].astype(F32) + dot(running, runs[origin + 1][:BLK])

        running = onward(middle_chip, running)
        back = returned(middle_chip, running)
        give(1, middle_chip, back)
        give(0, middle_chip + 1, running)
        for origin in range(middle_chip, 0, -1):
            back = known[origin] + dot(back, part_of(origin, 2 * AFFINE, BLK))
            give(1, origin - 1, back)
            ahead = 2 * middle_chip - origin + 1
            if ahead < chips:
                running = onward(ahead, running) if ahead < chips - 1 else running
                if ahead < chips - 1:
                    give(1, ahead, returned(ahead, running))
                    give(0, ahead + 1, running)
        got[1] = outflows[0]

    @pl.when(jnp.logical_not(at_hub) & (chip > 0))
    def _():
        result_copy(0, 1, 0).wait_recv()

    inflow = got[0].astype(F32)
    middle = dot(inflow, pair[0, :BLK]) + pair[0, BLK:AFFINE].astype(F32)
    centre = pair[1, AFFINE + BLK : 2 * AFFINE].astype(F32) + dot(
        middle, pair[1, AFFINE : AFFINE + BLK]
    )

    @pl.when(jnp.logical_not(at_hub) & (chip < chips - 1))
    def _():
        result_copy(1, 1, 0).wait_recv()

    outflow = got[1].astype(F32)
    centre = centre + dot(got[1], pair[1, 2 * AFFINE :])
    inflow = jnp.where(core == 0, inflow, middle)
    outflow = jnp.where(core == 0, centre, outflow)
    flows = jnp.concatenate([inflow, outflow], axis=1).astype(BF16)
    for k in range(ROWS):
        response = jnp.concatenate([bwd[k, :BLK], bwd[k, AFFINE:]], axis=0)
        solved = bwd_values[k] + dot(flows, response)
        solution_ref[k] = solved
        rows[k] = solved.astype(BF16)

    rim_copies = [
        pltpu.make_async_remote_copy(
            src_ref=rows.at[pl.ds(ROWS - RIM, RIM)],
            dst_ref=rim.at[pl.ds(0, RIM)],
            send_sem=rim_send.at[0],
            recv_sem=rim_recv.at[0],
            device_id=part_up,
            device_id_type=MESH,
        ),
        pltpu.make_async_remote_copy(
            src_ref=rows.at[pl.ds(0, RIM)],
            dst_ref=rim.at[pl.ds(RIM, RIM)],
            send_sem=rim_send.at[1],
            recv_sem=rim_recv.at[1],
            device_id=part_down,
            device_id_type=MESH,
        ),
    ]
    @pl.when(part < parts - 1)
    def _():
        rim_copies[0].start()

    @pl.when(part > 0)
    def _():
        rim_copies[1].start()

    last_copy.wait_recv()
    edges_before = (inflow - dot(rows[0], last_in[...])) * has_before
    edges = jnp.stack([edges_before, outflow * has_after]).astype(BF16)
    rows[pl.ds(ROWS, 2)] = edges
    for copy in loads[6:]:
        copy.wait()
    totals = []
    for k in range(ROWS):
        lows = [rows[jnp.where(lower_index[m, k] == k, ROWS, lower_index[m, k])] for m in range(3)]
        highs = [
            rows[jnp.where(upper_index[m, k] == k, ROWS + 1, upper_index[m, k])] for m in range(3)
        ]
        total = dot(rows[k], diag[k])
        total = total + dot(jnp.concatenate(lows, axis=1), lower[k].reshape(3 * BLK, BLK))
        total = total + dot(jnp.concatenate(highs, axis=1), upper[k].reshape(3 * BLK, BLK))
        product_ref[k] = total

    @pl.when(part > 0)
    def _():
        rim_copies[0].wait_recv()

    @pl.when(part < parts - 1)
    def _():
        rim_copies[1].wait_recv()

    for k in range(ROWS):
        sources = jnp.concatenate([rim[halo_index[h, k]] for h in range(2)], axis=1)
        product_ref[k] = product_ref[k] + dot(sources, halo[k].reshape(2 * BLK, BLK))

    pair_onward.wait_send()
    pair_back.wait_send()
    last_copy.wait_send()

    @pl.when(part < parts - 1)
    def _():
        rim_copies[0].wait_send()

    @pl.when(part > 0)
    def _():
        rim_copies[1].wait_send()

    for member, kind in groups:

        @pl.when(member)
        def _(kind=kind):
            element_copy(chip, core, *extent(kind)).wait_send()

    @pl.when(at_hub)
    def _():
        for kind in range(2):
            for target in range(1 - kind, chips - kind):
                for copy in result_copies(kind, target):
                    copy.wait_send()


def on_device(sections, parts, rhs, inverse, diag, lower, upper, halo, low_index, up_index, halo_index):
    chips = sections // 2
    hbm = pl.BlockSpec(memory_space=pl.ANY)
    vmem = pl.BlockSpec(memory_space=pltpu.VMEM)
    dma = pltpu.SemaphoreType.DMA
    return pl.pallas_call(
        functools.partial(kernel, sections, parts),
        out_shape=(
            pltpu.VMEM(rhs.shape, F32),
            pltpu.VMEM(rhs.shape, F32),
        ),
        in_specs=[hbm] * 9,
        out_specs=(vmem, vmem),
        scratch_shapes=[
            pltpu.SMEM(low_index.T.shape, jnp.int32),
            pltpu.SMEM(up_index.T.shape, jnp.int32),
            pltpu.SMEM(halo_index.T.shape, jnp.int32),
            pltpu.VMEM(rhs.shape, F32),
            pltpu.VMEM(inverse.shape, BF16),
            pltpu.VMEM(diag.shape, BF16),
            pltpu.VMEM(lower.shape, BF16),
            pltpu.VMEM(upper.shape, BF16),
            pltpu.VMEM(halo.shape, BF16),
            pltpu.VMEM((ROWS + 1, AFFINE, BLK), BF16),
            pltpu.VMEM((ROWS, AFFINE, BLK), F32),
            pltpu.VMEM((ROWS + 1, WIDE, BLK), BF16),
            pltpu.VMEM((ROWS, NRHS, BLK), F32),
            pltpu.VMEM((2, ELEMENT, BLK), BF16),
            pltpu.VMEM((ELEMENT, BLK), BF16),
            pltpu.VMEM((chips, ELEMENT, BLK), BF16),
            pltpu.VMEM((chips, NRHS, BLK), BF16),
            pltpu.VMEM((chips, NRHS, BLK), BF16),
            pltpu.VMEM((2, NRHS, BLK), BF16),
            pltpu.VMEM((BLK, BLK), BF16),
            pltpu.VMEM((BLK, BLK), BF16),
            pltpu.VMEM((ROWS + 2, NRHS, BLK), BF16),
            pltpu.VMEM((2 * RIM, NRHS, BLK), BF16),
            dma((9,)),
            dma((2,)),
            dma((2,)),
            dma((1,)),
            dma((chips, 2)),
            dma((chips, 2, 2)),
            dma((2,)),
            dma((1,)),
            dma((1,)),
            dma((2,)),
            dma((2,)),
        ],
        compiler_params=pltpu.CompilerParams(collective_id=0, has_side_effects=True),
        name="block_ilu_apply",
    )(low_index.T, up_index.T, halo_index.T, rhs, inverse, diag, lower, upper, halo)


def solution(mesh):
    row = ("section", "dom")
    in_specs = (
        P(row, None, None),
        P(row, None, None),
        P(row, None, None),
        P(row, None, None, None),
        P(row, None, None, None),
        P(row, None, None, None),
        P(row, None),
        P(row, None),
        P(row, None),
    )
    out_specs = (P(row, None, None), P(row, None, None))
    body = functools.partial(on_device, mesh.shape["section"], mesh.shape["dom"])
    return jax.shard_map(
        body, mesh=mesh, in_specs=in_specs, out_specs=out_specs, check_vma=False
    )
```

```python
import functools

import jax
import jax.numpy as jnp
from jax import lax
from jax.experimental import pallas as pl
from jax.experimental.pallas import tpu as pltpu
from jax.sharding import PartitionSpec as P

F32 = jnp.float32
BF16 = jnp.bfloat16
MESH = pl.DeviceIdType.MESH
ROWS = 8
BLK = 128
NRHS = 32
RIM = 4
AFFINE = BLK + NRHS
WIDE = AFFINE + BLK
ELEMENT = AFFINE + WIDE


def dot(left, right):
    return jnp.dot(left.astype(BF16), right, preferred_element_type=F32)


def joined_onward(left, right):
    through = dot(left[:AFFINE], right[:BLK])
    return jnp.concatenate(
        [through[:BLK], through[BLK:] + right[BLK:AFFINE].astype(F32)], axis=0
    ).astype(BF16)


def joined_back(onward, back, right):
    through = dot(onward, right[:BLK])
    through = [through[:BLK], through[BLK:] + right[BLK:AFFINE].astype(F32)]
    through = [part.astype(BF16) for part in through]
    if right.shape[0] > AFFINE:
        through.append(right[AFFINE:])
    through = dot(jnp.concatenate(through, axis=0), back[AFFINE:])
    affine = through[:AFFINE] + back[:AFFINE].astype(F32)
    if right.shape[0] == AFFINE:
        return affine.astype(BF16)
    return jnp.concatenate([affine, through[AFFINE:]], axis=0).astype(BF16)


def kernel(
    sections,
    parts,
    lower_index_hbm,
    upper_index_hbm,
    halo_index_hbm,
    rhs_hbm,
    inverse_hbm,
    diag_hbm,
    lower_hbm,
    upper_hbm,
    halo_hbm,
    solution_ref,
    product_ref,
    lower_index,
    upper_index,
    halo_index,
    rhs,
    inverse,
    diag,
    lower,
    upper,
    halo,
    fwd,
    fwd_wide,
    bwd,
    bwd_values,
    pair,
    whole,
    elements,
    inflows,
    outflows,
    got,
    last_own,
    last_in,
    rows,
    rim,
    load_sem,
    pair_send,
    pair_recv,
    element_send,
    element_recv,
    result_send,
    got_recv,
    last_send,
    last_recv,
    rim_send,
    rim_recv,
):
    chips = sections // 2
    middle_chip = chips // 2
    section = lax.axis_index("section")
    part = lax.axis_index("dom")
    core = lax.rem(section, 2)
    chip = lax.div(section, 2)
    sibling = (section + 1 - 2 * core, part)
    at_hub = section == 1
    hub_device = (1, part)
    beyond = (lax.rem(section + 2 * core - 1 + sections, sections), part)
    following = (lax.rem(section + 1, sections), part)
    part_up = (section, lax.min(part + 1, parts - 1))
    part_down = (section, lax.max(part - 1, 0))

    loads = []
    for place, (source, target) in enumerate(
        (
            (lower_index_hbm, lower_index),
            (lower_hbm, lower),
            (inverse_hbm, inverse),
            (rhs_hbm, rhs),
            (upper_index_hbm, upper_index),
            (upper_hbm, upper),
            (halo_index_hbm, halo_index),
            (diag_hbm, diag),
            (halo_hbm, halo),
        )
    ):
        copy = pltpu.make_async_copy(source, target, load_sem.at[place])
        copy.start()
        loads.append(copy)

    barrier = pltpu.get_barrier_semaphore()
    for device in (sibling, beyond):
        pl.semaphore_signal(barrier, inc=1, device_id=device, device_id_type=MESH)

    @pl.when(at_hub)
    def _():
        for other in range(sections):
            if other != 1:
                pl.semaphore_signal(barrier, inc=1, device_id=(other, part), device_id_type=MESH)

    @pl.when(jnp.logical_not(at_hub))
    def _():
        pl.semaphore_signal(barrier, inc=1, device_id=hub_device, device_id_type=MESH)

    @pl.when(part < parts - 1)
    def _():
        pl.semaphore_signal(barrier, inc=1, device_id=part_up, device_id_type=MESH)

    @pl.when(part > 0)
    def _():
        pl.semaphore_signal(barrier, inc=1, device_id=part_down, device_id_type=MESH)

    @pl.when(part == 0)
    def _():
        rim[pl.ds(0, RIM)] = jnp.zeros((RIM, NRHS, BLK), BF16)

    @pl.when(part == parts - 1)
    def _():
        rim[pl.ds(RIM, RIM)] = jnp.zeros((RIM, NRHS, BLK), BF16)

    @pl.when(chip == 0)
    def _():
        got[0] = jnp.zeros((NRHS, BLK), BF16)

    @pl.when(chip == chips - 1)
    def _():
        got[1] = jnp.zeros((NRHS, BLK), BF16)

    spread = lax.broadcasted_iota(jnp.int32, (BLK, BLK), 0)
    identity = (spread == lax.broadcasted_iota(jnp.int32, (BLK, BLK), 1)).astype(F32)
    has_before = (section > 0).astype(F32)
    has_after = (section < sections - 1).astype(F32)
    fwd[ROWS, :BLK] = (identity * has_before).astype(BF16)
    fwd[ROWS, BLK:] = jnp.zeros((NRHS, BLK), BF16)
    bwd[ROWS, :AFFINE] = jnp.zeros((AFFINE, BLK), BF16)
    bwd[ROWS, AFFINE:] = (identity * has_after).astype(BF16)

    for copy in loads[:4]:
        copy.wait()
    for k in range(ROWS):
        folded = dot(lower[k].reshape(3 * BLK, BLK), inverse[k])
        base = jnp.concatenate([folded[:BLK] * -has_before, dot(rhs[k], inverse[k])], axis=0)
        slots = [jnp.where(lower_index[m, k] == k, ROWS, lower_index[m, k]) for m in (1, 2)]
        sources = jnp.concatenate([fwd[slot] for slot in slots], axis=1)
        wide = base - dot(sources, folded[BLK:].astype(BF16))
        fwd_wide[k] = wide
        fwd[k] = wide.astype(BF16)
    pair[core, :AFFINE] = fwd[ROWS - 1]

    partners = jnp.where(at_hub, sections + 1, 3) + (part < parts - 1).astype(jnp.int32) + (part > 0).astype(jnp.int32)
    pl.semaphore_wait(barrier, partners)

    def pair_copy(piece, low, high):
        return pltpu.make_async_remote_copy(
            src_ref=pair.at[core, pl.ds(low, high - low)],
            dst_ref=pair.at[core, pl.ds(low, high - low)],
            send_sem=pair_send.at[piece],
            recv_sem=pair_recv.at[piece],
            device_id=sibling,
            device_id_type=MESH,
        )

    pair_onward = pair_copy(0, 0, AFFINE)
    pair_back = pair_copy(1, AFFINE, ELEMENT)
    pair_onward.start()

    for copy in loads[4:6]:
        copy.wait()
    for k in range(ROWS - 1, -1, -1):
        folded = dot(upper[k].reshape(3 * BLK, BLK), inverse[k])
        if k == ROWS - 1:
            last_own[...] = (folded[:BLK] + folded[BLK : 2 * BLK] + folded[2 * BLK :]).astype(BF16)
            last_copy = pltpu.make_async_remote_copy(
                src_ref=last_own,
                dst_ref=last_in,
                send_sem=last_send.at[0],
                recv_sem=last_recv.at[0],
                device_id=following,
                device_id_type=MESH,
            )
            last_copy.start()
        base = jnp.concatenate([fwd_wide[k], folded[:BLK] * -has_after], axis=0)
        slots = [jnp.where(upper_index[m, k] == k, ROWS, upper_index[m, k]) for m in (1, 2)]
        sources = jnp.concatenate([bwd[slot] for slot in slots], axis=1)
        wide = base - dot(sources, folded[BLK:].astype(BF16))
        bwd_values[k] = wide[BLK:AFFINE]
        bwd[k] = wide.astype(BF16)
    pair[core, AFFINE:] = bwd[0]
    pair_back.start()

    def element_copy(origin, half, kind, low, size):
        place = pl.ds(pl.multiple_of(low + size * half, 16), size)
        return pltpu.make_async_remote_copy(
            src_ref=whole.at[place],
            dst_ref=elements.at[origin, place],
            send_sem=element_send.at[kind],
            recv_sem=element_recv.at[origin, half, kind],
            device_id=hub_device,
            device_id_type=MESH,
        )

    def extent(kind, last):
        if kind == 0:
            return 0, AFFINE // 2
        return AFFINE, AFFINE // 2 if last else WIDE // 2

    between = (chip > 0) & (chip < chips - 1)
    groups = ((between, 0, False), (between, 1, False), (chip == chips - 1, 1, True))

    def send_element(wanted, action):
        for member, kind, last in groups:
            if kind == wanted:
                copy = element_copy(chip, core, kind, *extent(kind, last))
                pl.when(member)(getattr(copy, action))

    pair_onward.wait_recv()
    whole[:AFFINE] = joined_onward(pair[0, :AFFINE], pair[1, :AFFINE])
    send_element(0, "start")
    pair_back.wait_recv()
    whole[AFFINE:] = joined_back(pair[0, :AFFINE], pair[0, AFFINE:], pair[1, AFFINE:])
    send_element(1, "start")

    def result_copy(kind, target, target_core):
        return pltpu.make_async_remote_copy(
            src_ref=(inflows, outflows)[kind].at[target],
            dst_ref=got.at[kind],
            send_sem=result_send.at[target, kind, target_core],
            recv_sem=got_recv.at[kind],
            device_id=(2 * target + target_core, part),
            device_id_type=MESH,
        )

    def result_copies(kind, target):
        return [
            result_copy(kind, target, target_core)
            for target_core in (0, 1)
            if (target, target_core) != (0, 1)
        ]

    @pl.when(at_hub)
    def _():
        def take(origin, kind):
            last = origin == chips - 1
            if kind == 1 or not last:
                for half in range(2):
                    element_copy(origin, half, kind, *extent(kind, last)).wait_recv()

        def part_of(origin, low, size):
            ref = elements.at[origin] if origin else whole
            return ref[low : low + size]

        def onward(origin, running):
            values = part_of(origin, BLK, NRHS).astype(F32)
            return values + dot(running, part_of(origin, 0, BLK)) if origin else values

        def give(kind, target, values):
            (inflows, outflows)[kind][target] = values.astype(BF16)
            for copy in result_copies(kind, target):
                copy.start()

        order = sorted(range(1, chips), key=lambda c: min(c, chips - c))
        for origin in order:
            take(origin, 0)
        running = None
        for origin in range(chips - 1):
            running = onward(origin, running)
            give(0, origin + 1, running)
        for origin in order[:-1]:
            take(origin, 1)
        runs = [None] * chips
        runs[-1] = part_of(chips - 1, AFFINE, AFFINE)
        for origin in range(chips - 2, middle_chip, -1):
            runs[origin] = joined_back(
                part_of(origin, 0, AFFINE), part_of(origin, AFFINE, WIDE), runs[origin + 1]
            )
        for origin in range(middle_chip, chips - 1):
            beyond_run = runs[origin + 1]
            outflow = beyond_run[BLK:].astype(F32) + dot(inflows[origin + 1], beyond_run[:BLK])
            give(1, origin, outflow)
        shifts = [None] * chips
        gains = [None] * chips
        for origin in range(middle_chip - 1, 0, -1):
            shift = part_of(origin, AFFINE + BLK, NRHS).astype(F32) + dot(
                inflows[origin], part_of(origin, AFFINE, BLK)
            )
            gain = part_of(origin, 2 * AFFINE, BLK)
            if origin < middle_chip - 1:
                shift = shift + dot(shifts[origin + 1], gain)
                gain = dot(gains[origin + 1], gain).astype(BF16)
            shifts[origin], gains[origin] = shift, gain

        take(middle_chip, 1)
        first = part_of(middle_chip, AFFINE + BLK, NRHS).astype(F32) + dot(
            jnp.concatenate([inflows[middle_chip], outflows[middle_chip]], axis=1),
            jnp.concatenate(
                [part_of(middle_chip, AFFINE, BLK), part_of(middle_chip, 2 * AFFINE, BLK)], axis=0
            ),
        )
        give(1, middle_chip - 1, first)
        for origin in range(middle_chip - 1, 0, -1):
            give(1, origin - 1, shifts[origin] + dot(first, gains[origin]))
        got[1] = outflows[0]

    @pl.when(jnp.logical_not(at_hub) & (chip > 0))
    def _():
        result_copy(0, 1, 0).wait_recv()

    inflow = got[0].astype(F32)
    middle = dot(inflow, pair[0, :BLK]) + pair[0, BLK:AFFINE].astype(F32)
    centre = pair[1, AFFINE + BLK : 2 * AFFINE].astype(F32) + dot(
        middle, pair[1, AFFINE : AFFINE + BLK]
    )

    @pl.when(jnp.logical_not(at_hub) & (chip < chips - 1))
    def _():
        result_copy(1, 1, 0).wait_recv()

    outflow = got[1].astype(F32)
    centre = centre + dot(got[1], pair[1, 2 * AFFINE :])
    inflow = jnp.where(core == 0, inflow, middle)
    outflow = jnp.where(core == 0, centre, outflow)
    flows = jnp.concatenate([inflow, outflow], axis=1).astype(BF16)
    for k in range(ROWS):
        response = jnp.concatenate([bwd[k, :BLK], bwd[k, AFFINE:]], axis=0)
        solved = bwd_values[k] + dot(flows, response)
        solution_ref[k] = solved
        rows[k] = solved.astype(BF16)

    rim_copies = [
        pltpu.make_async_remote_copy(
            src_ref=rows.at[pl.ds(ROWS - RIM, RIM)],
            dst_ref=rim.at[pl.ds(0, RIM)],
            send_sem=rim_send.at[0],
            recv_sem=rim_recv.at[0],
            device_id=part_up,
            device_id_type=MESH,
        ),
        pltpu.make_async_remote_copy(
            src_ref=rows.at[pl.ds(0, RIM)],
            dst_ref=rim.at[pl.ds(RIM, RIM)],
            send_sem=rim_send.at[1],
            recv_sem=rim_recv.at[1],
            device_id=part_down,
            device_id_type=MESH,
        ),
    ]
    @pl.when(part < parts - 1)
    def _():
        rim_copies[0].start()

    @pl.when(part > 0)
    def _():
        rim_copies[1].start()

    last_copy.wait_recv()
    edges_before = (inflow - dot(rows[0], last_in[...])) * has_before
    edges = jnp.stack([edges_before, outflow * has_after]).astype(BF16)
    rows[pl.ds(ROWS, 2)] = edges
    for copy in loads[6:]:
        copy.wait()
    totals = []
    for k in range(ROWS):
        lows = [rows[jnp.where(lower_index[m, k] == k, ROWS, lower_index[m, k])] for m in range(3)]
        highs = [
            rows[jnp.where(upper_index[m, k] == k, ROWS + 1, upper_index[m, k])] for m in range(3)
        ]
        total = dot(rows[k], diag[k])
        total = total + dot(jnp.concatenate(lows, axis=1), lower[k].reshape(3 * BLK, BLK))
        total = total + dot(jnp.concatenate(highs, axis=1), upper[k].reshape(3 * BLK, BLK))
        product_ref[k] = total

    @pl.when(part > 0)
    def _():
        rim_copies[0].wait_recv()

    @pl.when(part < parts - 1)
    def _():
        rim_copies[1].wait_recv()

    for k in range(ROWS):
        sources = jnp.concatenate([rim[halo_index[h, k]] for h in range(2)], axis=1)
        product_ref[k] = product_ref[k] + dot(sources, halo[k].reshape(2 * BLK, BLK))

    pair_onward.wait_send()
    pair_back.wait_send()
    last_copy.wait_send()

    @pl.when(part < parts - 1)
    def _():
        rim_copies[0].wait_send()

    @pl.when(part > 0)
    def _():
        rim_copies[1].wait_send()

    for kind in range(2):
        send_element(kind, "wait_send")

    @pl.when(at_hub)
    def _():
        for kind in range(2):
            for target in range(1 - kind, chips - kind):
                for copy in result_copies(kind, target):
                    copy.wait_send()


def store(solved, product, solution_ref, product_ref, sems):
    copies = [
        pltpu.make_async_copy(solved, solution_ref, sems.at[0]),
        pltpu.make_async_copy(product, product_ref, sems.at[1]),
    ]
    for copy in copies:
        copy.start()
    for copy in copies:
        copy.wait()


def on_device(sections, parts, rhs, inverse, diag, lower, upper, halo, low_index, up_index, halo_index):
    chips = sections // 2
    hbm = pl.BlockSpec(memory_space=pl.ANY)
    vmem = pl.BlockSpec(memory_space=pltpu.VMEM)
    dma = pltpu.SemaphoreType.DMA
    solved, product = pl.pallas_call(
        functools.partial(kernel, sections, parts),
        out_shape=(
            pltpu.VMEM(rhs.shape, F32),
            pltpu.VMEM(rhs.shape, F32),
        ),
        in_specs=[hbm] * 9,
        out_specs=(vmem, vmem),
        scratch_shapes=[
            pltpu.SMEM(low_index.T.shape, jnp.int32),
            pltpu.SMEM(up_index.T.shape, jnp.int32),
            pltpu.SMEM(halo_index.T.shape, jnp.int32),
            pltpu.VMEM(rhs.shape, F32),
            pltpu.VMEM(inverse.shape, BF16),
            pltpu.VMEM(diag.shape, BF16),
            pltpu.VMEM(lower.shape, BF16),
            pltpu.VMEM(upper.shape, BF16),
            pltpu.VMEM(halo.shape, BF16),
            pltpu.VMEM((ROWS + 1, AFFINE, BLK), BF16),
            pltpu.VMEM((ROWS, AFFINE, BLK), F32),
            pltpu.VMEM((ROWS + 1, WIDE, BLK), BF16),
            pltpu.VMEM((ROWS, NRHS, BLK), F32),
            pltpu.VMEM((2, ELEMENT, BLK), BF16),
            pltpu.VMEM((ELEMENT, BLK), BF16),
            pltpu.VMEM((chips, ELEMENT, BLK), BF16),
            pltpu.VMEM((chips, NRHS, BLK), BF16),
            pltpu.VMEM((chips, NRHS, BLK), BF16),
            pltpu.VMEM((2, NRHS, BLK), BF16),
            pltpu.VMEM((BLK, BLK), BF16),
            pltpu.VMEM((BLK, BLK), BF16),
            pltpu.VMEM((ROWS + 2, NRHS, BLK), BF16),
            pltpu.VMEM((2 * RIM, NRHS, BLK), BF16),
            dma((9,)),
            dma((2,)),
            dma((2,)),
            dma((2,)),
            dma((chips, 2, 2)),
            dma((chips, 2, 2)),
            dma((2,)),
            dma((1,)),
            dma((1,)),
            dma((2,)),
            dma((2,)),
        ],
        compiler_params=pltpu.CompilerParams(collective_id=0, has_side_effects=True),
        name="block_ilu_apply",
    )(low_index.T, up_index.T, halo_index.T, rhs, inverse, diag, lower, upper, halo)
    solved = pltpu.with_memory_space_constraint(solved, pltpu.VMEM)
    product = pltpu.with_memory_space_constraint(product, pltpu.VMEM)
    return pl.pallas_call(
        store,
        out_shape=(jax.ShapeDtypeStruct(rhs.shape, F32),) * 2,
        in_specs=[vmem] * 2,
        out_specs=(hbm, hbm),
        scratch_shapes=[dma((2,))],
        name="store_outputs",
    )(solved, product)


def solution(mesh):
    row = ("section", "dom")
    in_specs = (
        P(row, None, None),
        P(row, None, None),
        P(row, None, None),
        P(row, None, None, None),
        P(row, None, None, None),
        P(row, None, None, None),
        P(row, None),
        P(row, None),
        P(row, None),
    )
    out_specs = (P(row, None, None), P(row, None, None))
    body = functools.partial(on_device, mesh.shape["section"], mesh.shape["dom"])
    return jax.shard_map(
        body, mesh=mesh, in_specs=in_specs, out_specs=out_specs, check_vma=False
    )
```

```python
import functools

import jax
import jax.numpy as jnp
from jax import lax
from jax.experimental import pallas as pl
from jax.experimental.pallas import tpu as pltpu
from jax.sharding import PartitionSpec as P

F32 = jnp.float32
BF16 = jnp.bfloat16
MESH = pl.DeviceIdType.MESH
ROWS = 8
BLK = 128
NRHS = 32
RIM = 4
AFFINE = BLK + NRHS
WIDE = AFFINE + BLK
ELEMENT = AFFINE + WIDE


def dot(left, right):
    return jnp.dot(left.astype(BF16), right, preferred_element_type=F32)


def joined_onward(left, right):
    through = dot(left[:AFFINE], right[:BLK])
    return jnp.concatenate(
        [through[:BLK], through[BLK:] + right[BLK:AFFINE].astype(F32)], axis=0
    ).astype(BF16)


def joined_back(onward, back, right):
    through = dot(onward, right[:BLK])
    through = [through[:BLK], through[BLK:] + right[BLK:AFFINE].astype(F32)]
    through = [part.astype(BF16) for part in through]
    if right.shape[0] > AFFINE:
        through.append(right[AFFINE:])
    through = dot(jnp.concatenate(through, axis=0), back[AFFINE:])
    affine = through[:AFFINE] + back[:AFFINE].astype(F32)
    if right.shape[0] == AFFINE:
        return affine.astype(BF16)
    return jnp.concatenate([affine, through[AFFINE:]], axis=0).astype(BF16)


def kernel(
    sections,
    parts,
    lower_index_hbm,
    upper_index_hbm,
    halo_index_hbm,
    rhs_hbm,
    inverse_hbm,
    diag_hbm,
    lower_hbm,
    upper_hbm,
    halo_hbm,
    solution_ref,
    product_ref,
    lower_index,
    upper_index,
    halo_index,
    rhs,
    inverse,
    diag,
    lower,
    upper,
    halo,
    fwd,
    fwd_wide,
    bwd,
    bwd_values,
    pair,
    whole,
    elements,
    inflows,
    outflows,
    got,
    last_own,
    last_in,
    rows,
    rim,
    load_sem,
    pair_send,
    pair_recv,
    element_send,
    element_recv,
    result_send,
    got_recv,
    last_send,
    last_recv,
    rim_send,
    rim_recv,
):
    chips = sections // 2
    middle_chip = chips // 2
    section = lax.axis_index("section")
    part = lax.axis_index("dom")
    core = lax.rem(section, 2)
    chip = lax.div(section, 2)
    sibling = (section + 1 - 2 * core, part)
    at_hub = section == 1
    hub_device = (1, part)
    beyond = (lax.rem(section + 2 * core - 1 + sections, sections), part)
    following = (lax.rem(section + 1, sections), part)
    part_up = (section, lax.min(part + 1, parts - 1))
    part_down = (section, lax.max(part - 1, 0))

    loads = []
    for place, (source, target) in enumerate(
        (
            (lower_index_hbm, lower_index),
            (lower_hbm.at[pl.ds(0, 3)], lower.at[pl.ds(0, 3)]),
            (inverse_hbm, inverse),
            (rhs_hbm, rhs),
            (lower_hbm.at[pl.ds(3, 5)], lower.at[pl.ds(3, 5)]),
            (upper_index_hbm, upper_index),
            (upper_hbm, upper),
            (halo_index_hbm, halo_index),
            (diag_hbm, diag),
            (halo_hbm, halo),
        )
    ):
        copy = pltpu.make_async_copy(source, target, load_sem.at[place])
        copy.start()
        loads.append(copy)

    barrier = pltpu.get_barrier_semaphore()
    for device in (sibling, beyond):
        pl.semaphore_signal(barrier, inc=1, device_id=device, device_id_type=MESH)

    @pl.when(at_hub)
    def _():
        for other in range(sections):
            if other != 1:
                pl.semaphore_signal(barrier, inc=1, device_id=(other, part), device_id_type=MESH)

    @pl.when(jnp.logical_not(at_hub))
    def _():
        pl.semaphore_signal(barrier, inc=1, device_id=hub_device, device_id_type=MESH)

    @pl.when(part < parts - 1)
    def _():
        pl.semaphore_signal(barrier, inc=1, device_id=part_up, device_id_type=MESH)

    @pl.when(part > 0)
    def _():
        pl.semaphore_signal(barrier, inc=1, device_id=part_down, device_id_type=MESH)

    @pl.when(part == 0)
    def _():
        rim[pl.ds(0, RIM)] = jnp.zeros((RIM, NRHS, BLK), BF16)

    @pl.when(part == parts - 1)
    def _():
        rim[pl.ds(RIM, RIM)] = jnp.zeros((RIM, NRHS, BLK), BF16)

    @pl.when(chip == 0)
    def _():
        got[0] = jnp.zeros((NRHS, BLK), BF16)

    @pl.when(chip == chips - 1)
    def _():
        got[1] = jnp.zeros((NRHS, BLK), BF16)

    spread = lax.broadcasted_iota(jnp.int32, (BLK, BLK), 0)
    identity = (spread == lax.broadcasted_iota(jnp.int32, (BLK, BLK), 1)).astype(F32)
    has_before = (section > 0).astype(F32)
    has_after = (section < sections - 1).astype(F32)
    fwd[ROWS, :BLK] = (identity * has_before).astype(BF16)
    fwd[ROWS, BLK:] = jnp.zeros((NRHS, BLK), BF16)
    bwd[ROWS, :AFFINE] = jnp.zeros((AFFINE, BLK), BF16)
    bwd[ROWS, AFFINE:] = (identity * has_after).astype(BF16)

    for copy in loads[:4]:
        copy.wait()
    for k in range(ROWS):
        if k == 3:
            loads[4].wait()
        folded = dot(lower[k].reshape(3 * BLK, BLK), inverse[k])
        base = jnp.concatenate([folded[:BLK] * -has_before, dot(rhs[k], inverse[k])], axis=0)
        slots = [jnp.where(lower_index[m, k] == k, ROWS, lower_index[m, k]) for m in (1, 2)]
        sources = jnp.concatenate([fwd[slot] for slot in slots], axis=1)
        wide = base - dot(sources, folded[BLK:].astype(BF16))
        fwd_wide[k] = wide
        fwd[k] = wide.astype(BF16)
    pair[core, :AFFINE] = fwd[ROWS - 1]

    partners = jnp.where(at_hub, sections + 1, 3) + (part < parts - 1).astype(jnp.int32) + (part > 0).astype(jnp.int32)
    pl.semaphore_wait(barrier, partners)

    def pair_copy(piece, low, high):
        return pltpu.make_async_remote_copy(
            src_ref=pair.at[core, pl.ds(low, high - low)],
            dst_ref=pair.at[core, pl.ds(low, high - low)],
            send_sem=pair_send.at[piece],
            recv_sem=pair_recv.at[piece],
            device_id=sibling,
            device_id_type=MESH,
        )

    pair_onward = pair_copy(0, 0, AFFINE)
    pair_back = pair_copy(1, AFFINE, ELEMENT)
    pair_onward.start()

    for copy in loads[5:7]:
        copy.wait()
    for k in range(ROWS - 1, -1, -1):
        folded = dot(upper[k].reshape(3 * BLK, BLK), inverse[k])
        if k == ROWS - 1:
            last_own[...] = (folded[:BLK] + folded[BLK : 2 * BLK] + folded[2 * BLK :]).astype(BF16)
            last_copy = pltpu.make_async_remote_copy(
                src_ref=last_own,
                dst_ref=last_in,
                send_sem=last_send.at[0],
                recv_sem=last_recv.at[0],
                device_id=following,
                device_id_type=MESH,
            )
            last_copy.start()
        base = jnp.concatenate([fwd_wide[k], folded[:BLK] * -has_after], axis=0)
        slots = [jnp.where(upper_index[m, k] == k, ROWS, upper_index[m, k]) for m in (1, 2)]
        sources = jnp.concatenate([bwd[slot] for slot in slots], axis=1)
        wide = base - dot(sources, folded[BLK:].astype(BF16))
        bwd_values[k] = wide[BLK:AFFINE]
        bwd[k] = wide.astype(BF16)
    pair[core, AFFINE:] = bwd[0]
    pair_back.start()

    def element_copy(origin, half, kind, low, size):
        place = pl.ds(pl.multiple_of(low + size * half, 16), size)
        return pltpu.make_async_remote_copy(
            src_ref=whole.at[place],
            dst_ref=elements.at[origin, place],
            send_sem=element_send.at[kind],
            recv_sem=element_recv.at[origin, half, kind],
            device_id=hub_device,
            device_id_type=MESH,
        )

    def extent(kind, last):
        if kind == 0:
            return 0, AFFINE // 2
        return AFFINE, AFFINE // 2 if last else WIDE // 2

    between = (chip > 0) & (chip < chips - 1)
    groups = ((between, 0, False), (between, 1, False), (chip == chips - 1, 1, True))

    def send_element(wanted, action):
        for member, kind, last in groups:
            if kind == wanted:
                copy = element_copy(chip, core, kind, *extent(kind, last))
                pl.when(member)(getattr(copy, action))

    pair_onward.wait_recv()
    whole[:AFFINE] = joined_onward(pair[0, :AFFINE], pair[1, :AFFINE])
    send_element(0, "start")
    pair_back.wait_recv()
    whole[AFFINE:] = joined_back(pair[0, :AFFINE], pair[0, AFFINE:], pair[1, AFFINE:])
    send_element(1, "start")

    def result_copy(kind, target, target_core):
        return pltpu.make_async_remote_copy(
            src_ref=(inflows, outflows)[kind].at[target],
            dst_ref=got.at[kind],
            send_sem=result_send.at[target, kind, target_core],
            recv_sem=got_recv.at[kind],
            device_id=(2 * target + target_core, part),
            device_id_type=MESH,
        )

    def result_copies(kind, target):
        return [
            result_copy(kind, target, target_core)
            for target_core in (0, 1)
            if (target, target_core) != (0, 1)
        ]

    @pl.when(at_hub)
    def _():
        def take(origin, kind):
            last = origin == chips - 1
            if kind == 1 or not last:
                for half in range(2):
                    element_copy(origin, half, kind, *extent(kind, last)).wait_recv()

        def part_of(origin, low, size):
            ref = elements.at[origin] if origin else whole
            return ref[low : low + size]

        def onward(origin, running):
            values = part_of(origin, BLK, NRHS).astype(F32)
            return values + dot(running, part_of(origin, 0, BLK)) if origin else values

        def give(kind, target, values):
            (inflows, outflows)[kind][target] = values.astype(BF16)
            for copy in result_copies(kind, target):
                copy.start()

        def known(origin):
            values = part_of(origin, AFFINE + BLK, NRHS).astype(F32)
            return values + dot(inflows[origin], part_of(origin, AFFINE, BLK))

        def first_of(origin):
            sources = jnp.concatenate([inflows[origin], outflows[origin]], axis=1)
            maps = [part_of(origin, AFFINE, BLK), part_of(origin, 2 * AFFINE, BLK)]
            values = part_of(origin, AFFINE + BLK, NRHS).astype(F32)
            return values + dot(sources, jnp.concatenate(maps, axis=0))

        running = None
        for origin in range(middle_chip):
            if origin:
                take(origin, 0)
            running = onward(origin, running)
            give(0, origin + 1, running)
        nearer = middle_chip - 1
        shifts = [None] * chips
        gains = [None] * chips
        for origin in range(1, nearer):
            take(origin, 1)
        for origin in range(nearer - 1, 0, -1):
            gain = part_of(origin, 2 * AFFINE, BLK)
            shift = known(origin)
            if origin < nearer - 1:
                shift = shift + dot(shifts[origin + 1], gain)
                gain = dot(gains[origin + 1], gain).astype(BF16)
            shifts[origin], gains[origin] = shift, gain
        for origin in range(chips - 1, middle_chip + 1, -1):
            take(origin, 0)
            take(origin, 1)
        if middle_chip + 1 < chips - 1:
            take(middle_chip + 1, 0)
        take(middle_chip, 0)
        for origin in range(middle_chip, chips - 1):
            running = onward(origin, running)
            give(0, origin + 1, running)
        for origin in range(chips - 1, middle_chip, -1):
            if origin == middle_chip + 1:
                take(origin, 1)
            give(1, origin - 1, first_of(origin) if origin < chips - 1 else known(origin))
        take(nearer, 1)
        shift = known(nearer)
        gain = part_of(nearer, 2 * AFFINE, BLK)
        ahead = jnp.concatenate([gain, shift.astype(BF16)], axis=0)
        for origin in range(1, nearer):
            through = dot(ahead, gains[origin])
            gains[origin] = through[:BLK].astype(BF16)
            shifts[origin] = shifts[origin] + through[BLK:]
        shifts[nearer], gains[nearer] = shift, gain

        take(middle_chip, 1)
        first = first_of(middle_chip)
        give(1, nearer, first)
        for origin in range(nearer, 0, -1):
            give(1, origin - 1, shifts[origin] + dot(first, gains[origin]))
        got[1] = outflows[0]

    @pl.when(jnp.logical_not(at_hub) & (chip > 0))
    def _():
        result_copy(0, 1, 0).wait_recv()

    inflow = got[0].astype(F32)
    middle = dot(inflow, pair[0, :BLK]) + pair[0, BLK:AFFINE].astype(F32)
    centre = pair[1, AFFINE + BLK : 2 * AFFINE].astype(F32) + dot(
        middle, pair[1, AFFINE : AFFINE + BLK]
    )

    @pl.when(jnp.logical_not(at_hub) & (chip < chips - 1))
    def _():
        result_copy(1, 1, 0).wait_recv()

    outflow = got[1].astype(F32)
    centre = centre + dot(got[1], pair[1, 2 * AFFINE :])
    inflow = jnp.where(core == 0, inflow, middle)
    outflow = jnp.where(core == 0, centre, outflow)
    flows = jnp.concatenate([inflow, outflow], axis=1).astype(BF16)
    rim_copies = [
        pltpu.make_async_remote_copy(
            src_ref=rows.at[pl.ds(ROWS - RIM, RIM)],
            dst_ref=rim.at[pl.ds(0, RIM)],
            send_sem=rim_send.at[0],
            recv_sem=rim_recv.at[0],
            device_id=part_up,
            device_id_type=MESH,
        ),
        pltpu.make_async_remote_copy(
            src_ref=rows.at[pl.ds(0, RIM)],
            dst_ref=rim.at[pl.ds(RIM, RIM)],
            send_sem=rim_send.at[1],
            recv_sem=rim_recv.at[1],
            device_id=part_down,
            device_id_type=MESH,
        ),
    ]
    def solve_rows(low, high):
        for k in range(low, high):
            response = jnp.concatenate([bwd[k, :BLK], bwd[k, AFFINE:]], axis=0)
            solved = bwd_values[k] + dot(flows, response)
            solution_ref[k] = solved
            rows[k] = solved.astype(BF16)

    solve_rows(0, RIM)
    pl.when(part > 0)(rim_copies[1].start)
    solve_rows(RIM, ROWS)
    pl.when(part < parts - 1)(rim_copies[0].start)

    last_copy.wait_recv()
    edges_before = (inflow - dot(rows[0], last_in[...])) * has_before
    edges = jnp.stack([edges_before, outflow * has_after]).astype(BF16)
    rows[pl.ds(ROWS, 2)] = edges
    for copy in loads[7:]:
        copy.wait()
    totals = []
    for k in range(ROWS):
        lows = [rows[jnp.where(lower_index[m, k] == k, ROWS, lower_index[m, k])] for m in range(3)]
        highs = [
            rows[jnp.where(upper_index[m, k] == k, ROWS + 1, upper_index[m, k])] for m in range(3)
        ]
        total = dot(rows[k], diag[k])
        total = total + dot(jnp.concatenate(lows, axis=1), lower[k].reshape(3 * BLK, BLK))
        total = total + dot(jnp.concatenate(highs, axis=1), upper[k].reshape(3 * BLK, BLK))
        product_ref[k] = total

    @pl.when(part > 0)
    def _():
        rim_copies[0].wait_recv()

    @pl.when(part < parts - 1)
    def _():
        rim_copies[1].wait_recv()

    for k in range(ROWS):
        sources = jnp.concatenate([rim[halo_index[h, k]] for h in range(2)], axis=1)
        product_ref[k] = product_ref[k] + dot(sources, halo[k].reshape(2 * BLK, BLK))

    pair_onward.wait_send()
    pair_back.wait_send()
    last_copy.wait_send()

    @pl.when(part < parts - 1)
    def _():
        rim_copies[0].wait_send()

    @pl.when(part > 0)
    def _():
        rim_copies[1].wait_send()

    for kind in range(2):
        send_element(kind, "wait_send")

    @pl.when(at_hub)
    def _():
        for kind in range(2):
            for target in range(1 - kind, chips - kind):
                for copy in result_copies(kind, target):
                    copy.wait_send()


def store(solved, product, solution_ref, product_ref, sems):
    copies = [
        pltpu.make_async_copy(solved, solution_ref, sems.at[0]),
        pltpu.make_async_copy(product, product_ref, sems.at[1]),
    ]
    for copy in copies:
        copy.start()
    for copy in copies:
        copy.wait()


def on_device(sections, parts, rhs, inverse, diag, lower, upper, halo, low_index, up_index, halo_index):
    chips = sections // 2
    hbm = pl.BlockSpec(memory_space=pl.ANY)
    vmem = pl.BlockSpec(memory_space=pltpu.VMEM)
    dma = pltpu.SemaphoreType.DMA
    solved, product = pl.pallas_call(
        functools.partial(kernel, sections, parts),
        out_shape=(
            pltpu.VMEM(rhs.shape, F32),
            pltpu.VMEM(rhs.shape, F32),
        ),
        in_specs=[hbm] * 9,
        out_specs=(vmem, vmem),
        scratch_shapes=[
            pltpu.SMEM(low_index.T.shape, jnp.int32),
            pltpu.SMEM(up_index.T.shape, jnp.int32),
            pltpu.SMEM(halo_index.T.shape, jnp.int32),
            pltpu.VMEM(rhs.shape, F32),
            pltpu.VMEM(inverse.shape, BF16),
            pltpu.VMEM(diag.shape, BF16),
            pltpu.VMEM(lower.shape, BF16),
            pltpu.VMEM(upper.shape, BF16),
            pltpu.VMEM(halo.shape, BF16),
            pltpu.VMEM((ROWS + 1, AFFINE, BLK), BF16),
            pltpu.VMEM((ROWS, AFFINE, BLK), F32),
            pltpu.VMEM((ROWS + 1, WIDE, BLK), BF16),
            pltpu.VMEM((ROWS, NRHS, BLK), F32),
            pltpu.VMEM((2, ELEMENT, BLK), BF16),
            pltpu.VMEM((ELEMENT, BLK), BF16),
            pltpu.VMEM((chips, ELEMENT, BLK), BF16),
            pltpu.VMEM((chips, NRHS, BLK), BF16),
            pltpu.VMEM((chips, NRHS, BLK), BF16),
            pltpu.VMEM((2, NRHS, BLK), BF16),
            pltpu.VMEM((BLK, BLK), BF16),
            pltpu.VMEM((BLK, BLK), BF16),
            pltpu.VMEM((ROWS + 2, NRHS, BLK), BF16),
            pltpu.VMEM((2 * RIM, NRHS, BLK), BF16),
            dma((10,)),
            dma((2,)),
            dma((2,)),
            dma((2,)),
            dma((chips, 2, 2)),
            dma((chips, 2, 2)),
            dma((2,)),
            dma((1,)),
            dma((1,)),
            dma((2,)),
            dma((2,)),
        ],
        compiler_params=pltpu.CompilerParams(collective_id=0, has_side_effects=True),
        name="block_ilu_apply",
    )(low_index.T, up_index.T, halo_index.T, rhs, inverse, diag, lower, upper, halo)
    solved = pltpu.with_memory_space_constraint(solved, pltpu.VMEM)
    product = pltpu.with_memory_space_constraint(product, pltpu.VMEM)
    return pl.pallas_call(
        store,
        out_shape=(jax.ShapeDtypeStruct(rhs.shape, F32),) * 2,
        in_specs=[vmem] * 2,
        out_specs=(hbm, hbm),
        scratch_shapes=[dma((2,))],
        name="store_outputs",
    )(solved, product)


def solution(mesh):
    row = ("section", "dom")
    in_specs = (
        P(row, None, None),
        P(row, None, None),
        P(row, None, None),
        P(row, None, None, None),
        P(row, None, None, None),
        P(row, None, None, None),
        P(row, None),
        P(row, None),
        P(row, None),
    )
    out_specs = (P(row, None, None), P(row, None, None))
    body = functools.partial(on_device, mesh.shape["section"], mesh.shape["dom"])
    return jax.shard_map(
        body, mesh=mesh, in_specs=in_specs, out_specs=out_specs, check_vma=False
    )
```

```python
import functools

import jax
import jax.numpy as jnp
from jax import lax
from jax.experimental import pallas as pl
from jax.experimental.pallas import tpu as pltpu
from jax.sharding import PartitionSpec as P

F32 = jnp.float32
BF16 = jnp.bfloat16
MESH = pl.DeviceIdType.MESH
ROWS = 8
BLK = 128
NRHS = 32
RIM = 4
AFFINE = BLK + NRHS
WIDE = AFFINE + BLK
ELEMENT = AFFINE + WIDE


def dot(left, right):
    return jnp.dot(left.astype(BF16), right, preferred_element_type=F32)


def joined_onward(left, right):
    through = dot(left[:AFFINE], right[:BLK])
    return jnp.concatenate(
        [through[:BLK], through[BLK:] + right[BLK:AFFINE].astype(F32)], axis=0
    ).astype(BF16)


def joined_back(onward, back, right):
    through = dot(onward, right[:BLK])
    through = [through[:BLK], through[BLK:] + right[BLK:AFFINE].astype(F32)]
    through = [part.astype(BF16) for part in through]
    if right.shape[0] > AFFINE:
        through.append(right[AFFINE:])
    through = dot(jnp.concatenate(through, axis=0), back[AFFINE:])
    affine = through[:AFFINE] + back[:AFFINE].astype(F32)
    if right.shape[0] == AFFINE:
        return affine.astype(BF16)
    return jnp.concatenate([affine, through[AFFINE:]], axis=0).astype(BF16)


def kernel(
    sections,
    parts,
    lower_index_hbm,
    upper_index_hbm,
    halo_index_hbm,
    rhs_hbm,
    inverse_hbm,
    diag_hbm,
    lower_hbm,
    upper_hbm,
    halo_hbm,
    solution_ref,
    product_ref,
    lower_index,
    upper_index,
    halo_index,
    rhs,
    inverse,
    diag,
    lower,
    upper,
    halo,
    fwd,
    fwd_wide,
    bwd,
    bwd_values,
    pair,
    whole,
    elements,
    inflows,
    outflows,
    got,
    last_own,
    last_in,
    rows,
    rim,
    load_sem,
    pair_send,
    pair_recv,
    element_send,
    element_recv,
    result_send,
    got_recv,
    last_send,
    last_recv,
    rim_send,
    rim_recv,
):
    chips = sections // 2
    middle_chip = chips // 2
    section = lax.axis_index("section")
    part = lax.axis_index("dom")
    core = lax.rem(section, 2)
    chip = lax.div(section, 2)
    sibling = (section + 1 - 2 * core, part)
    at_hub = section == 1
    hub_device = (1, part)
    beyond = (lax.rem(section + 2 * core - 1 + sections, sections), part)
    following = (lax.rem(section + 1, sections), part)
    part_up = (section, lax.min(part + 1, parts - 1))
    part_down = (section, lax.max(part - 1, 0))

    loads = []
    for place, (source, target) in enumerate(
        (
            (lower_index_hbm, lower_index),
            (lower_hbm.at[pl.ds(0, 3)], lower.at[pl.ds(0, 3)]),
            (inverse_hbm, inverse),
            (rhs_hbm, rhs),
            (lower_hbm.at[pl.ds(3, 5)], lower.at[pl.ds(3, 5)]),
            (upper_index_hbm, upper_index),
            (upper_hbm, upper),
            (halo_index_hbm, halo_index),
            (diag_hbm, diag),
            (halo_hbm, halo),
        )
    ):
        copy = pltpu.make_async_copy(source, target, load_sem.at[place])
        copy.start()
        loads.append(copy)

    barrier = pltpu.get_barrier_semaphore()
    for device in (sibling, beyond):
        pl.semaphore_signal(barrier, inc=1, device_id=device, device_id_type=MESH)

    @pl.when(at_hub)
    def _():
        for other in range(sections):
            if other != 1:
                pl.semaphore_signal(barrier, inc=1, device_id=(other, part), device_id_type=MESH)

    @pl.when(jnp.logical_not(at_hub))
    def _():
        pl.semaphore_signal(barrier, inc=1, device_id=hub_device, device_id_type=MESH)

    @pl.when(part < parts - 1)
    def _():
        pl.semaphore_signal(barrier, inc=1, device_id=part_up, device_id_type=MESH)

    @pl.when(part > 0)
    def _():
        pl.semaphore_signal(barrier, inc=1, device_id=part_down, device_id_type=MESH)

    @pl.when(part == 0)
    def _():
        rim[pl.ds(0, RIM)] = jnp.zeros((RIM, NRHS, BLK), BF16)

    @pl.when(part == parts - 1)
    def _():
        rim[pl.ds(RIM, RIM)] = jnp.zeros((RIM, NRHS, BLK), BF16)

    @pl.when(section == 0)
    def _():
        last_in[...] = jnp.zeros((BLK, BLK), BF16)

    @pl.when(chip == 0)
    def _():
        got[0] = jnp.zeros((NRHS, BLK), BF16)

    @pl.when(chip == chips - 1)
    def _():
        got[1] = jnp.zeros((NRHS, BLK), BF16)

    spread = lax.broadcasted_iota(jnp.int32, (BLK, BLK), 0)
    identity = (spread == lax.broadcasted_iota(jnp.int32, (BLK, BLK), 1)).astype(F32)
    has_before = (section > 0).astype(F32)
    has_after = (section < sections - 1).astype(F32)
    fwd[ROWS, :BLK] = (identity * has_before).astype(BF16)
    fwd[ROWS, BLK:] = jnp.zeros((NRHS, BLK), BF16)
    bwd[ROWS, :AFFINE] = jnp.zeros((AFFINE, BLK), BF16)
    bwd[ROWS, AFFINE:] = (identity * has_after).astype(BF16)

    for copy in loads[:4]:
        copy.wait()
    for k in range(ROWS):
        if k == 3:
            loads[4].wait()
        folded = dot(lower[k].reshape(3 * BLK, BLK), inverse[k])
        base = jnp.concatenate([folded[:BLK] * -has_before, dot(rhs[k], inverse[k])], axis=0)
        slots = [jnp.where(lower_index[m, k] == k, ROWS, lower_index[m, k]) for m in (1, 2)]
        sources = jnp.concatenate([fwd[slot] for slot in slots], axis=1)
        wide = base - dot(sources, folded[BLK:].astype(BF16))
        fwd_wide[k] = wide
        fwd[k] = wide.astype(BF16)
    pair[core, :AFFINE] = fwd[ROWS - 1]

    partners = jnp.where(at_hub, sections + 1, 3) + (part < parts - 1).astype(jnp.int32) + (part > 0).astype(jnp.int32)
    pl.semaphore_wait(barrier, partners)

    def pair_copy(piece, low, high):
        return pltpu.make_async_remote_copy(
            src_ref=pair.at[core, pl.ds(low, high - low)],
            dst_ref=pair.at[core, pl.ds(low, high - low)],
            send_sem=pair_send.at[piece],
            recv_sem=pair_recv.at[piece],
            device_id=sibling,
            device_id_type=MESH,
        )

    pair_onward = pair_copy(0, 0, AFFINE)
    pair_back = pair_copy(1, AFFINE, ELEMENT)
    pair_onward.start()

    for copy in loads[5:7]:
        copy.wait()
    for k in range(ROWS - 1, -1, -1):
        folded = dot(upper[k].reshape(3 * BLK, BLK), inverse[k])
        if k == ROWS - 1:
            last_own[...] = (folded[:BLK] + folded[BLK : 2 * BLK] + folded[2 * BLK :]).astype(BF16)
            last_copy = pltpu.make_async_remote_copy(
                src_ref=last_own,
                dst_ref=last_in,
                send_sem=last_send.at[0],
                recv_sem=last_recv.at[0],
                device_id=following,
                device_id_type=MESH,
            )
            pl.when(section < sections - 1)(last_copy.start)
        base = jnp.concatenate([fwd_wide[k], folded[:BLK] * -has_after], axis=0)
        slots = [jnp.where(upper_index[m, k] == k, ROWS, upper_index[m, k]) for m in (1, 2)]
        sources = jnp.concatenate([bwd[slot] for slot in slots], axis=1)
        wide = base - dot(sources, folded[BLK:].astype(BF16))
        bwd_values[k] = wide[BLK:AFFINE]
        bwd[k] = wide.astype(BF16)
    pair[core, AFFINE:] = bwd[0]
    pair_back.start()

    def element_copy(origin, half, kind, low, size):
        place = pl.ds(pl.multiple_of(low + size * half, 16), size)
        return pltpu.make_async_remote_copy(
            src_ref=whole.at[place],
            dst_ref=elements.at[origin, place],
            send_sem=element_send.at[kind],
            recv_sem=element_recv.at[origin, half, kind],
            device_id=hub_device,
            device_id_type=MESH,
        )

    def extent(kind, last):
        if kind == 0:
            return 0, AFFINE // 2
        return AFFINE, AFFINE // 2 if last else WIDE // 2

    between = (chip > 0) & (chip < chips - 1)
    groups = ((between, 0, False), (between, 1, False), (chip == chips - 1, 1, True))

    def send_element(wanted, action):
        for member, kind, last in groups:
            if kind == wanted:
                copy = element_copy(chip, core, kind, *extent(kind, last))
                pl.when(member)(getattr(copy, action))

    pair_onward.wait_recv()
    whole[:AFFINE] = joined_onward(pair[0, :AFFINE], pair[1, :AFFINE])
    send_element(0, "start")
    pair_back.wait_recv()
    whole[AFFINE:] = joined_back(pair[0, :AFFINE], pair[0, AFFINE:], pair[1, AFFINE:])
    send_element(1, "start")

    def result_copy(kind, target, target_core):
        return pltpu.make_async_remote_copy(
            src_ref=(inflows, outflows)[kind].at[target],
            dst_ref=got.at[kind],
            send_sem=result_send.at[target, kind, target_core],
            recv_sem=got_recv.at[kind],
            device_id=(2 * target + target_core, part),
            device_id_type=MESH,
        )

    def result_copies(kind, target):
        return [
            result_copy(kind, target, target_core)
            for target_core in (0, 1)
            if (target, target_core) != (0, 1)
        ]

    @pl.when(at_hub)
    def _():
        def take(origin, kind):
            last = origin == chips - 1
            if kind == 1 or not last:
                for half in range(2):
                    element_copy(origin, half, kind, *extent(kind, last)).wait_recv()

        def part_of(origin, low, size):
            ref = elements.at[origin] if origin else whole
            return ref[low : low + size]

        def onward(origin, running):
            values = part_of(origin, BLK, NRHS).astype(F32)
            return values + dot(running, part_of(origin, 0, BLK)) if origin else values

        def give(kind, target, values):
            (inflows, outflows)[kind][target] = values.astype(BF16)
            for copy in result_copies(kind, target):
                copy.start()

        def known(origin):
            values = part_of(origin, AFFINE + BLK, NRHS).astype(F32)
            return values + dot(inflows[origin], part_of(origin, AFFINE, BLK))

        def first_of(origin):
            sources = jnp.concatenate([inflows[origin], outflows[origin]], axis=1)
            maps = [part_of(origin, AFFINE, BLK), part_of(origin, 2 * AFFINE, BLK)]
            values = part_of(origin, AFFINE + BLK, NRHS).astype(F32)
            return values + dot(sources, jnp.concatenate(maps, axis=0))

        running = None
        for origin in range(middle_chip):
            if origin:
                take(origin, 0)
            running = onward(origin, running)
            give(0, origin + 1, running)
        nearer = middle_chip - 1
        shifts = [None] * chips
        gains = [None] * chips
        for origin in range(1, nearer):
            take(origin, 1)
        for origin in range(nearer - 1, 0, -1):
            gain = part_of(origin, 2 * AFFINE, BLK)
            shift = known(origin)
            if origin < nearer - 1:
                shift = shift + dot(shifts[origin + 1], gain)
                gain = dot(gains[origin + 1], gain).astype(BF16)
            shifts[origin], gains[origin] = shift, gain
        for origin in range(chips - 1, middle_chip + 1, -1):
            take(origin, 0)
            take(origin, 1)
        if middle_chip + 1 < chips - 1:
            take(middle_chip + 1, 0)
        take(middle_chip, 0)
        for origin in range(middle_chip, chips - 1):
            running = onward(origin, running)
            give(0, origin + 1, running)
        for origin in range(chips - 1, middle_chip, -1):
            if origin == middle_chip + 1:
                take(origin, 1)
            give(1, origin - 1, first_of(origin) if origin < chips - 1 else known(origin))
        take(nearer, 1)
        shift = known(nearer)
        gain = part_of(nearer, 2 * AFFINE, BLK)
        ahead = jnp.concatenate([gain, shift.astype(BF16)], axis=0)
        for origin in range(1, nearer):
            through = dot(ahead, gains[origin])
            gains[origin] = through[:BLK].astype(BF16)
            shifts[origin] = shifts[origin] + through[BLK:]
        shifts[nearer], gains[nearer] = shift, gain

        take(middle_chip, 1)
        first = first_of(middle_chip)
        give(1, nearer, first)
        for origin in range(nearer, 0, -1):
            give(1, origin - 1, shifts[origin] + dot(first, gains[origin]))
        got[1] = outflows[0]

    @pl.when(jnp.logical_not(at_hub) & (chip > 0))
    def _():
        result_copy(0, 1, 0).wait_recv()

    inflow = got[0].astype(F32)
    middle = dot(inflow, pair[0, :BLK]) + pair[0, BLK:AFFINE].astype(F32)
    centre = pair[1, AFFINE + BLK : 2 * AFFINE].astype(F32) + dot(
        middle, pair[1, AFFINE : AFFINE + BLK]
    )

    @pl.when(jnp.logical_not(at_hub) & (chip < chips - 1))
    def _():
        result_copy(1, 1, 0).wait_recv()

    outflow = got[1].astype(F32)
    centre = centre + dot(got[1], pair[1, 2 * AFFINE :])
    inflow = jnp.where(core == 0, inflow, middle)
    outflow = jnp.where(core == 0, centre, outflow)
    flows = jnp.concatenate([inflow, outflow], axis=1).astype(BF16)
    rim_copies = [
        pltpu.make_async_remote_copy(
            src_ref=rows.at[pl.ds(ROWS - RIM, RIM)],
            dst_ref=rim.at[pl.ds(0, RIM)],
            send_sem=rim_send.at[0],
            recv_sem=rim_recv.at[0],
            device_id=part_up,
            device_id_type=MESH,
        ),
        pltpu.make_async_remote_copy(
            src_ref=rows.at[pl.ds(0, RIM)],
            dst_ref=rim.at[pl.ds(RIM, RIM)],
            send_sem=rim_send.at[1],
            recv_sem=rim_recv.at[1],
            device_id=part_down,
            device_id_type=MESH,
        ),
    ]
    def solve_rows(low, high):
        for k in range(low, high):
            response = jnp.concatenate([bwd[k, :BLK], bwd[k, AFFINE:]], axis=0)
            solved = bwd_values[k] + dot(flows, response)
            solution_ref[k] = solved
            rows[k] = solved.astype(BF16)

    solve_rows(0, RIM)
    pl.when(part > 0)(rim_copies[1].start)
    solve_rows(RIM, ROWS)
    pl.when(part < parts - 1)(rim_copies[0].start)

    pl.when(section > 0)(last_copy.wait_recv)
    edges_before = (inflow - dot(rows[0], last_in[...])) * has_before
    edges = jnp.stack([edges_before, outflow * has_after]).astype(BF16)
    rows[pl.ds(ROWS, 2)] = edges
    for copy in loads[7:]:
        copy.wait()
    totals = []
    for k in range(ROWS):
        lows = [rows[jnp.where(lower_index[m, k] == k, ROWS, lower_index[m, k])] for m in range(3)]
        highs = [
            rows[jnp.where(upper_index[m, k] == k, ROWS + 1, upper_index[m, k])] for m in range(3)
        ]
        total = dot(rows[k], diag[k])
        total = total + dot(jnp.concatenate(lows, axis=1), lower[k].reshape(3 * BLK, BLK))
        total = total + dot(jnp.concatenate(highs, axis=1), upper[k].reshape(3 * BLK, BLK))
        product_ref[k] = total

    @pl.when(part > 0)
    def _():
        rim_copies[0].wait_recv()

    @pl.when(part < parts - 1)
    def _():
        rim_copies[1].wait_recv()

    for k in range(ROWS):
        sources = jnp.concatenate([rim[halo_index[h, k]] for h in range(2)], axis=1)
        product_ref[k] = product_ref[k] + dot(sources, halo[k].reshape(2 * BLK, BLK))

    pair_onward.wait_send()
    pair_back.wait_send()
    pl.when(section < sections - 1)(last_copy.wait_send)

    @pl.when(part < parts - 1)
    def _():
        rim_copies[0].wait_send()

    @pl.when(part > 0)
    def _():
        rim_copies[1].wait_send()

    for kind in range(2):
        send_element(kind, "wait_send")

    @pl.when(at_hub)
    def _():
        for kind in range(2):
            for target in range(1 - kind, chips - kind):
                for copy in result_copies(kind, target):
                    copy.wait_send()


def store(solved, product, solution_ref, product_ref, sems):
    copies = [
        pltpu.make_async_copy(solved, solution_ref, sems.at[0]),
        pltpu.make_async_copy(product, product_ref, sems.at[1]),
    ]
    for copy in copies:
        copy.start()
    for copy in copies:
        copy.wait()


def on_device(sections, parts, rhs, inverse, diag, lower, upper, halo, low_index, up_index, halo_index):
    chips = sections // 2
    hbm = pl.BlockSpec(memory_space=pl.ANY)
    vmem = pl.BlockSpec(memory_space=pltpu.VMEM)
    dma = pltpu.SemaphoreType.DMA
    solved, product = pl.pallas_call(
        functools.partial(kernel, sections, parts),
        out_shape=(
            pltpu.VMEM(rhs.shape, F32),
            pltpu.VMEM(rhs.shape, F32),
        ),
        in_specs=[hbm] * 9,
        out_specs=(vmem, vmem),
        scratch_shapes=[
            pltpu.SMEM(low_index.T.shape, jnp.int32),
            pltpu.SMEM(up_index.T.shape, jnp.int32),
            pltpu.SMEM(halo_index.T.shape, jnp.int32),
            pltpu.VMEM(rhs.shape, F32),
            pltpu.VMEM(inverse.shape, BF16),
            pltpu.VMEM(diag.shape, BF16),
            pltpu.VMEM(lower.shape, BF16),
            pltpu.VMEM(upper.shape, BF16),
            pltpu.VMEM(halo.shape, BF16),
            pltpu.VMEM((ROWS + 1, AFFINE, BLK), BF16),
            pltpu.VMEM((ROWS, AFFINE, BLK), F32),
            pltpu.VMEM((ROWS + 1, WIDE, BLK), BF16),
            pltpu.VMEM((ROWS, NRHS, BLK), F32),
            pltpu.VMEM((2, ELEMENT, BLK), BF16),
            pltpu.VMEM((ELEMENT, BLK), BF16),
            pltpu.VMEM((chips, ELEMENT, BLK), BF16),
            pltpu.VMEM((chips, NRHS, BLK), BF16),
            pltpu.VMEM((chips, NRHS, BLK), BF16),
            pltpu.VMEM((2, NRHS, BLK), BF16),
            pltpu.VMEM((BLK, BLK), BF16),
            pltpu.VMEM((BLK, BLK), BF16),
            pltpu.VMEM((ROWS + 2, NRHS, BLK), BF16),
            pltpu.VMEM((2 * RIM, NRHS, BLK), BF16),
            dma((10,)),
            dma((2,)),
            dma((2,)),
            dma((2,)),
            dma((chips, 2, 2)),
            dma((chips, 2, 2)),
            dma((2,)),
            dma((1,)),
            dma((1,)),
            dma((2,)),
            dma((2,)),
        ],
        compiler_params=pltpu.CompilerParams(collective_id=0, has_side_effects=True),
        name="block_ilu_apply",
    )(low_index.T, up_index.T, halo_index.T, rhs, inverse, diag, lower, upper, halo)
    solved = pltpu.with_memory_space_constraint(solved, pltpu.VMEM)
    product = pltpu.with_memory_space_constraint(product, pltpu.VMEM)
    return pl.pallas_call(
        store,
        out_shape=(jax.ShapeDtypeStruct(rhs.shape, F32),) * 2,
        in_specs=[vmem] * 2,
        out_specs=(hbm, hbm),
        scratch_shapes=[dma((2,))],
        name="store_outputs",
    )(solved, product)


def solution(mesh):
    row = ("section", "dom")
    in_specs = (
        P(row, None, None),
        P(row, None, None),
        P(row, None, None),
        P(row, None, None, None),
        P(row, None, None, None),
        P(row, None, None, None),
        P(row, None),
        P(row, None),
        P(row, None),
    )
    out_specs = (P(row, None, None), P(row, None, None))
    body = functools.partial(on_device, mesh.shape["section"], mesh.shape["dom"])
    return jax.shard_map(
        body, mesh=mesh, in_specs=in_specs, out_specs=out_specs, check_vma=False
    )
```
